128 devices in a mesh: row: 16 (over z_hi, x, core), col: 8 (over y, z_lo).
Axes of the slice: x: 4, y: 4, z: 4 (z_hi: 2, z_lo: 2; z = z_hi * 2 + z_lo), core: 2. Of those that a mesh axis runs over, the one named last changes fastest.
Arguments:
- before_scan: float32 [4, 4096, 8192], P(None, 'row', 'col'), may hold values from -40 to 40
- after_scan: float32 [4, 4096, 8192], P(None, 'row', 'col'), may hold values from -40 to 40
- drift_offsets: int32 [2, 4, 16, 8], P(None, None, 'row', 'col'), may hold values from -128 to 128, as said below
- drift_fractions: int32 [2, 4, 16, 8], P(None, None, 'row', 'col'), may hold values from 0 to 255
Outputs:
- band_field: float32 [4, 4096, 8192], P(None, 'row', 'col')
- slope_field: float32 [4, 4096, 8192], P(None, 'row', 'col')
- surface_params: float32 [2, 4], replicated
The draws below stay inside these ranges and needn't reach their ends.
Inputs may be any that keep to these rules, and one draw needn't show every extreme that they name: `drift_offsets`: for every scan and tile, the cells a tile reads (its own cells shifted by its offsets, widened by one row and column before and two after) lie inside the window. In every scan the first tile has offsets 128, 128 and the last tile minus 128, minus 128.
All inputs are finite; a program needn't handle non-finite values.
Results may differ from the reference program's by a relative error of at most 0.00014.
Values sent between devices are 32-bit elements; how exact they have to be, the bound alone decides.
No kernel may reach another device: no remote copies, remote signals or barrier semaphores. Data moves between devices by JAX's collectives and lax.ppermute only.
A program may use at most 128 MiB of HBM per device.

```python
import math
import jax
import jax.numpy as jnp
from jax import lax

SCANS = 4
TR = 256
TC = 1024
LS = 5
SR = 4
LCUT = 1600
BLOCK = 16
DRIFT = 128
NR = 4096
NC = 8192
N_ROW = 16
N_COL = 8


wave_terms = 6


def scale_profile(row_power, col_power):
    row_frac = jnp.arange(NR, dtype=jnp.float32) / NR
    col_frac = jnp.arange(NC, dtype=jnp.float32) / NC
    return jnp.power(row_power, row_frac)[:, None] * jnp.power(col_power, col_frac)[None, :]


def rough_part(key):
    rough_noise = jnp.clip(jax.random.normal(key, (SCANS, NR, NC), jnp.float32), -4.0, 4.0)
    return 0.2 * rough_noise * scale_profile(10.0, 3.0)


def wave_part(key):
    subkeys = jax.random.split(key, 4)
    amplitude = jnp.clip(0.6 * jax.random.normal(subkeys[0], (SCANS, wave_terms), jnp.float32), -1.5, 1.5)
    row_waves = jax.random.uniform(subkeys[1], (SCANS, wave_terms), jnp.float32, -2.0, 2.0)
    col_waves = jax.random.uniform(subkeys[2], (SCANS, wave_terms), jnp.float32, -2.0, 2.0)
    phases = jax.random.uniform(subkeys[3], (SCANS, wave_terms), jnp.float32, 0.0, 2.0 * math.pi)
    row_frac = jnp.arange(NR, dtype=jnp.float32) / NR
    col_frac = jnp.arange(NC, dtype=jnp.float32) / NC
    waviness = jnp.zeros((SCANS, NR, NC), jnp.float32)
    for wave_index in range(wave_terms):
        argument = 2.0 * math.pi * (row_waves[:, wave_index, None, None] * row_frac[None, :, None] + col_waves[:, wave_index, None, None] * col_frac[None, None, :]) + phases[:, wave_index, None, None]
        waviness = waviness + amplitude[:, wave_index, None, None] * jnp.cos(argument)
    return waviness


def draw_before_scan(key, part):
    heights = rough_part(jax.random.fold_in(key, 1)) + wave_part(jax.random.fold_in(key, 2))
    return heights


def draw_after_scan(key, part):
    return rough_part(jax.random.fold_in(key, 3)) + wave_part(jax.random.fold_in(key, 4))


def draw_drift_offsets(key, part):
    drawn_values = jax.random.randint(jax.random.fold_in(key, 5), (2, SCANS, N_ROW, N_COL), -DRIFT, DRIFT + 1, dtype=jnp.int32)
    row_tile = jnp.arange(N_ROW, dtype=jnp.int32)[None, None, :, None]
    col_tile = jnp.arange(N_COL, dtype=jnp.int32)[None, None, None, :]
    full_shape = (1, SCANS, N_ROW, N_COL)
    row_low = jnp.broadcast_to(jnp.where(row_tile == 0, 1, -DRIFT), full_shape)
    row_high = jnp.broadcast_to(jnp.where(row_tile == N_ROW - 1, -2, DRIFT), full_shape)
    col_low = jnp.broadcast_to(jnp.where(col_tile == 0, 1, -DRIFT), full_shape)
    col_high = jnp.broadcast_to(jnp.where(col_tile == N_COL - 1, -2, DRIFT), full_shape)
    bounded = jnp.clip(drawn_values, jnp.concatenate([row_low, col_low], axis=0), jnp.concatenate([row_high, col_high], axis=0))
    bounded = bounded.at[:, :, 0, 0].set(DRIFT)
    return bounded.at[:, :, N_ROW - 1, N_COL - 1].set(-DRIFT).astype(jnp.int32)


def place_ends(result, key, low, top_value):
    extent = result.shape
    index_at = [jax.random.randint(jax.random.fold_in(key, axis), (), 0, extent[axis]) for axis in range(len(extent))]
    result = result.at[tuple(index_at)].set(low)
    longest = extent.index(max(extent))
    index_at[longest] = (index_at[longest] + 1) % extent[longest]
    return result.at[tuple(index_at)].set(top_value)


def setup_inputs(seed: int = 0) -> dict:
    splits = jax.random.split(jax.random.key(seed), 5)
    before_scan = draw_before_scan(jax.random.fold_in(splits[4], 71), 0)
    after_scan = draw_after_scan(jax.random.fold_in(splits[4], 71), 0)
    drift_offsets = draw_drift_offsets(jax.random.fold_in(splits[4], 71), 0)
    drift_fractions = place_ends(jax.random.randint(splits[3], (2, SCANS, N_ROW, N_COL), 0, 256), jax.random.fold_in(splits[3], 1), 0, 255).astype(jnp.int32)
    return dict(before_scan=before_scan, after_scan=after_scan, drift_offsets=drift_offsets, drift_fractions=drift_fractions)


ALPHA = math.sqrt(math.log(2.0) / math.pi)
SPACING = 0.5
EPSILON = 1e-06
HIGHEST = lax.Precision.HIGHEST

def cubic_weights(fraction):
    position = fraction.astype(jnp.float32) / 256.0
    square = position * position
    cube_term = square * position
    return (0.5 * (2.0 * square - cube_term - position), 0.5 * (3.0 * cube_term - 5.0 * square + 2.0), 0.5 * (4.0 * square - 3.0 * cube_term + position), 0.5 * (cube_term - square))

def interpolate(window, row_taps, col_taps):
    height = window.shape[0] - 3
    length = window.shape[1] - 3
    across = row_taps[0] * window[0:height] + row_taps[1] * window[1:height + 1] + row_taps[2] * window[2:height + 2] + row_taps[3] * window[3:height + 3]
    return col_taps[0] * across[:, 0:length] + col_taps[1] * across[:, 1:length + 1] + col_taps[2] * across[:, 2:length + 2] + col_taps[3] * across[:, 3:length + 3]

def resample(after_scan, drift_offsets, drift_fractions):
    margin = DRIFT + 2
    padded = jnp.pad(after_scan, ((0, 0), (margin, margin), (margin, margin)))
    scan_id = jnp.broadcast_to(jnp.arange(SCANS, dtype=jnp.int32)[:, None, None], (SCANS, N_ROW, N_COL))
    row_start = jnp.arange(N_ROW, dtype=jnp.int32)[None, :, None] * TR + (margin - 1) + drift_offsets[0]
    col_start = jnp.arange(N_COL, dtype=jnp.int32)[None, None, :] * TC + (margin - 1) + drift_offsets[1]
    row_taps = jnp.stack(cubic_weights(drift_fractions[0]), axis=-1).reshape(-1, 4)
    col_taps = jnp.stack(cubic_weights(drift_fractions[1]), axis=-1).reshape(-1, 4)

    def one_tile(scan_index, row_first, col_first, row_weights, col_weights):
        window = lax.dynamic_slice(padded, (scan_index, row_first, col_first), (1, TR + 3, TC + 3))[0]
        return interpolate(window, row_weights, col_weights)
    resampled = jax.vmap(one_tile)(scan_id.reshape(-1), row_start.reshape(-1).astype(jnp.int32), col_start.reshape(-1).astype(jnp.int32), row_taps, col_taps)
    resampled = resampled.reshape(SCANS, N_ROW, N_COL, TR, TC).transpose(0, 1, 3, 2, 4)
    return resampled.reshape(SCANS, NR, NC)

def short_taps():
    return [math.exp(-math.pi * (offset / (ALPHA * LS)) ** 2) for offset in range(-SR, SR + 1)]

def short_filter(surface):
    kernel_taps = short_taps()
    padded = jnp.pad(surface, ((0, 0), (0, 0), (SR, SR)))
    inside = jnp.pad(jnp.ones((NC,), jnp.float32), (SR, SR))
    summed = kernel_taps[0] * padded[:, :, 0:NC]
    weight = kernel_taps[0] * inside[0:NC]
    for offset in range(1, 2 * SR + 1):
        summed = summed + kernel_taps[offset] * padded[:, :, offset:offset + NC]
        weight = weight + kernel_taps[offset] * inside[offset:offset + NC]
    across = summed / weight
    padded = jnp.pad(across, ((0, 0), (SR, SR), (0, 0)))
    inside = jnp.pad(jnp.ones((NR,), jnp.float32), (SR, SR))
    summed = kernel_taps[0] * padded[:, 0:NR, :]
    weight = kernel_taps[0] * inside[0:NR]
    for offset in range(1, 2 * SR + 1):
        summed = summed + kernel_taps[offset] * padded[:, offset:offset + NR, :]
        weight = weight + kernel_taps[offset] * inside[offset:offset + NR]
    return summed / weight[:, None]

def coarse_means(surface):
    return surface.reshape(SCANS, NR // BLOCK, BLOCK, NC // BLOCK, BLOCK).mean(axis=(2, 4))

def gauss_block(source, target):
    distance = ((source[:, None] - target[None, :]) * BLOCK).astype(jnp.float32) / (ALPHA * LCUT)
    return jnp.exp(-math.pi * distance * distance)

def upsample_matrix(fine_index, coarse_index, coarse_count):
    numerator = 2 * fine_index + 1 - BLOCK
    lower_index = numerator // (2 * BLOCK)
    fraction = (numerator - lower_index * (2 * BLOCK)).astype(jnp.float32) / (2.0 * BLOCK)
    outside = (lower_index < 0) | (lower_index >= coarse_count - 1)
    fraction = jnp.where(outside, jnp.zeros_like(fraction), fraction)
    lower_index = jnp.clip(lower_index, 0, coarse_count - 1)
    first_part = (coarse_index[None, :] == lower_index[:, None]).astype(jnp.float32) * (1.0 - fraction)[:, None]
    second_part = (coarse_index[None, :] == (lower_index + 1)[:, None]).astype(jnp.float32) * fraction[:, None]
    return first_part + second_part

def slopes(surface):
    padded = jnp.pad(surface, ((0, 0), (1, 1), (1, 1)))
    column_index = jnp.arange(NC, dtype=jnp.int32)
    row_index = jnp.arange(NR, dtype=jnp.int32)
    column_mask = ((column_index >= 1) & (column_index <= NC - 2)).astype(jnp.float32)
    row_mask = ((row_index >= 1) & (row_index <= NR - 2)).astype(jnp.float32)
    along_cols = (padded[:, 1:-1, 2:] - padded[:, 1:-1, :-2]) / (2.0 * SPACING) * column_mask
    along_rows = (padded[:, 2:, 1:-1] - padded[:, :-2, 1:-1]) / (2.0 * SPACING) * row_mask[:, None]
    return along_cols * along_cols + along_rows * along_rows

def reference(before_scan, after_scan, drift_offsets, drift_fractions):
    shifted = resample(after_scan, drift_offsets, drift_fractions)
    difference = before_scan - shifted
    smooth = short_filter(difference)
    coarse = coarse_means(smooth)
    coarse_cols = jnp.arange(NC // BLOCK, dtype=jnp.int32)
    col_matrix = gauss_block(coarse_cols, coarse_cols)
    along = jnp.einsum('sak,kb->sab', coarse, col_matrix, precision=HIGHEST) / lax.optimization_barrier(jnp.sum(col_matrix, axis=0))
    coarse_rows = jnp.arange(NR // BLOCK, dtype=jnp.int32)
    row_matrix = gauss_block(coarse_rows, coarse_rows)
    wavy_coarse = jnp.einsum('ak,skb->sab', row_matrix, along, precision=HIGHEST) / lax.optimization_barrier(jnp.sum(row_matrix, axis=1))[:, None]
    row_up = upsample_matrix(jnp.arange(NR, dtype=jnp.int32), coarse_rows, NR // BLOCK)
    col_up = upsample_matrix(jnp.arange(NC, dtype=jnp.int32), coarse_cols, NC // BLOCK)
    row_mixed = jnp.einsum('pa,sab->spb', row_up, wavy_coarse, precision=HIGHEST)
    waviness = jnp.einsum('spb,qb->spq', row_mixed, col_up, precision=HIGHEST)
    band_field = smooth - waviness
    slope_field = slopes(band_field)
    height_sq = lax.optimization_barrier(jnp.sum(band_field * band_field, axis=(1, 2)))
    slope_sum = lax.optimization_barrier(jnp.sum(slope_field, axis=(1, 2)))
    surface_params = jnp.sqrt(jnp.stack([height_sq, slope_sum]) / (NR * NC) + EPSILON)
    return (band_field, slope_field, surface_params)
```

```python
import math

import jax
import jax.numpy as jnp
from jax import lax
from jax.experimental import pallas as pl
from jax.experimental.pallas import tpu as pltpu
from jax.sharding import PartitionSpec as P

LS = 5
SR = 4
LCUT = 1600
BLOCK = 16
ALPHA = math.sqrt(math.log(2.0) / math.pi)
EPSILON = 1e-06
HIGHEST = lax.Precision.HIGHEST
HALO = 136
EDGE = 8
LANES = 128
TAPS = [math.exp(-math.pi * (k / (ALPHA * LS)) ** 2) for k in range(-SR, SR + 1)]
VMEM_LIMIT = 56 * 1024 * 1024


def lane_iota(rows):
    return lax.broadcasted_iota(jnp.int32, (rows, LANES), 1)


def pack_kernel(offs_ref, x_ref, top_ref, bot_ref, left_ref, right_ref):
    s = pl.program_id(0)
    shift = offs_ref[1, s].astype(jnp.float32)
    rows, cols = x_ref.shape[1], x_ref.shape[2]
    for j in range(cols // LANES):
        sl = slice(j * LANES, (j + 1) * LANES)
        top_ref[0, j] = x_ref[0, 0:HALO, sl]
        bot_ref[0, j] = x_ref[0, rows - HALO : rows, sl]
    top_ref[0, 0, HALO - 1 : HALO, :] = jnp.full((1, LANES), shift, jnp.float32)
    bot_ref[0, 0, 0:1, :] = jnp.full((1, LANES), shift, jnp.float32)
    left_ref[0] = x_ref[0, :, 0:256].T[0:HALO, :]
    right_ref[0] = x_ref[0, :, cols - 256 : cols].T[256 - HALO : 256, :]


def pack(after, offs):
    scans, rows, cols = after.shape
    n_tiles = cols // LANES
    return pl.pallas_call(
        pack_kernel,
        grid=(scans,),
        in_specs=[
            pl.BlockSpec(memory_space=pltpu.SMEM),
            pl.BlockSpec((1, rows, cols), lambda s: (s, 0, 0)),
        ],
        out_specs=[
            pl.BlockSpec((1, n_tiles, HALO, LANES), lambda s: (s, 0, 0, 0)),
            pl.BlockSpec((1, n_tiles, HALO, LANES), lambda s: (s, 0, 0, 0)),
            pl.BlockSpec((1, HALO, rows), lambda s: (s, 0, 0)),
            pl.BlockSpec((1, HALO, rows), lambda s: (s, 0, 0)),
        ],
        out_shape=[
            jax.ShapeDtypeStruct((scans, n_tiles, HALO, LANES), jnp.float32),
            jax.ShapeDtypeStruct((scans, n_tiles, HALO, LANES), jnp.float32),
            jax.ShapeDtypeStruct((scans, HALO, rows), jnp.float32),
            jax.ShapeDtypeStruct((scans, HALO, rows), jnp.float32),
        ],
        name="pack",
    )(offs, after)


def scalar_taps(fraction):
    t = fraction.astype(jnp.float32) * (1.0 / 256.0)
    t2 = t * t
    t3 = t2 * t
    return (
        0.5 * (2.0 * t2 - t3 - t),
        0.5 * (3.0 * t3 - 5.0 * t2 + 2.0),
        0.5 * (4.0 * t2 - 3.0 * t3 + t),
        0.5 * (t3 - t2),
    )


RB = 16


def resample_kernel(
    offs_ref, fracs_ref, cm_ref, rm_ref, hc_ref,
    after, before, up, dn, lcols, rcols, cup, cdn,
    diff_out, edge_l, edge_r, y_ref,
    win, stage, bef, dif, sem, bsem, osem,
):
    scans = win.shape[0]
    rows, cols = bef.shape[1], bef.shape[2]
    n_out = cols // LANES
    left = 2 * LANES

    def copies(s):
        return [
            (after.at[s, :, pl.ds(j * LANES, LANES)], win.at[s, 2 + j, pl.ds(HALO, rows), :])
            for j in range(n_out)
        ] + [
            (up.at[s], win.at[s, pl.ds(2, n_out), pl.ds(0, HALO), :]),
            (dn.at[s], win.at[s, pl.ds(2, n_out), pl.ds(HALO + rows, HALO), :]),
            (lcols.at[s], stage.at[s, 0, pl.ds(256 - HALO, HALO), :]),
            (rcols.at[s], stage.at[s, 1, pl.ds(0, HALO), :]),
            (cup.at[s], stage.at[s, 2, pl.ds(256 - HALO, HALO), :]),
            (cup.at[s], stage.at[s, 3, pl.ds(0, HALO), :]),
            (cdn.at[s], stage.at[s, 4, pl.ds(256 - HALO, HALO), :]),
            (cdn.at[s], stage.at[s, 5, pl.ds(0, HALO), :]),
        ]

    for s in range(scans):
        for n, (a, b) in enumerate(copies(s)):
            pltpu.make_async_copy(a, b, sem.at[s, n]).start()
        pltpu.make_async_copy(before.at[s], bef.at[s], bsem.at[s]).start()

    def one_scan(s, carry):
        for n, (a, b) in enumerate(copies(s)):
            pltpu.make_async_copy(a, b, sem.at[s, n]).wait()
        pltpu.make_async_copy(before.at[s], bef.at[s], bsem.at[s]).wait()
        dr = offs_ref[0, s]
        dc = offs_ref[1, s]

        def put(slot, first_tile, row0, part):
            flipped = stage[s, slot].T
            for h in range(2):
                win[s, first_tile + h, row0 : row0 + part.stop - part.start, :] = flipped[
                    part, h * LANES : (h + 1) * LANES
                ]

        def put_side(first_tile, slots):
            put(slots[0], first_tile, HALO, slice(0, rows))

            @pl.when(dr <= 0)
            def _():
                put(slots[1], first_tile, 0, slice(rows - HALO, rows))

            @pl.when(dr >= -1)
            def _():
                put(slots[2], first_tile, HALO + rows, slice(0, HALO))

        @pl.when(dc <= 0)
        def _():
            put_side(0, (0, 2, 4))

        @pl.when(dc >= -1)
        def _():
            put_side(2 + n_out, (1, 3, 5))

        rt = scalar_taps(fracs_ref[0, s])
        ct = scalar_taps(fracs_ref[1, s])
        r0 = HALO + dr - 1
        c0 = left + dc - 1
        k = lax.div(c0, LANES)
        r = c0 - k * LANES
        back = lax.rem(LANES - r, LANES)
        lane = lane_iota(RB)
        keep = lane < LANES - r

        def block(i, carry):
            p0 = i * RB
            first = r0 + p0
            tiles = []
            for j in range(n_out + 2):
                acc = rt[0] * win[s, k + j, pl.ds(first, RB), :]
                for a in range(1, 4):
                    acc = acc + rt[a] * win[s, k + j, pl.ds(first + a, RB), :]
                tiles.append(pltpu.roll(acc, back, 1))
            al = [jnp.where(keep, tiles[j], tiles[j + 1]) for j in range(n_out + 1)]
            outs = [ct[0] * al[j] for j in range(n_out)]
            for b in range(1, 4):
                rolled = [pltpu.roll(t, LANES - b, 1) for t in al]
                m = lane < LANES - b
                for j in range(n_out):
                    outs[j] = outs[j] + ct[b] * jnp.where(m, rolled[j], rolled[j + 1])
            po = pl.multiple_of(p0, RB)
            for j in range(n_out):
                sl = slice(j * LANES, (j + 1) * LANES)
                dif[s, pl.ds(po, RB), sl] = bef[s, pl.ds(po, RB), sl] - outs[j]
            return carry

        lax.fori_loop(0, rows // RB, block, 0)
        pltpu.make_async_copy(dif.at[s], diff_out.at[s], osem.at[s]).start()
        d = dif[s]
        edge_l[s] = d[:, 0:LANES].T[0:EDGE]
        edge_r[s] = d[:, cols - LANES : cols].T[LANES - EDGE : LANES]
        t1 = jnp.dot(d, cm_ref[...], precision=HIGHEST, preferred_element_type=jnp.float32)
        c1 = jnp.dot(rm_ref[...], t1, precision=HIGHEST, preferred_element_type=jnp.float32)
        for t in range(y_ref.shape[0]):
            y_ref[t, s] = jnp.dot(
                c1, hc_ref[:, t * LANES : (t + 1) * LANES],
                precision=HIGHEST, preferred_element_type=jnp.float32,
            )
        return carry

    lax.fori_loop(0, scans, one_scan, 0)
    for s in range(scans):
        pltpu.make_async_copy(dif.at[s], diff_out.at[s], osem.at[s]).wait()


def resample(offs, fracs, cm, rm, hc, after, before, up, dn, lcols, rcols, cup, cdn):
    scans, rows, cols = after.shape
    n_col = hc.shape[1] // LANES
    ext = rm.shape[0]
    anywhere = pl.BlockSpec(memory_space=pl.ANY)
    vmem = pl.BlockSpec(memory_space=pltpu.VMEM)
    smem = pl.BlockSpec(memory_space=pltpu.SMEM)
    return pl.pallas_call(
        resample_kernel,
        in_specs=[smem, smem, vmem, vmem, vmem] + [anywhere] * 8,
        out_specs=[anywhere, vmem, vmem, vmem],
        out_shape=[
            jax.ShapeDtypeStruct((scans, rows, cols), jnp.float32),
            jax.ShapeDtypeStruct((scans, EDGE, rows), jnp.float32),
            jax.ShapeDtypeStruct((scans, EDGE, rows), jnp.float32),
            jax.ShapeDtypeStruct((n_col, scans, ext, LANES), jnp.float32),
        ],
        scratch_shapes=[
            pltpu.VMEM((scans, cols // LANES + 4, 2 * HALO + rows, LANES), jnp.float32),
            pltpu.VMEM((scans, 6, 256, rows), jnp.float32),
            pltpu.VMEM((scans, rows, cols), jnp.float32),
            pltpu.VMEM((scans, rows, cols), jnp.float32),
            pltpu.SemaphoreType.DMA((scans, cols // LANES + 8)),
            pltpu.SemaphoreType.DMA((scans,)),
            pltpu.SemaphoreType.DMA((scans,)),
        ],
        compiler_params=pltpu.CompilerParams(vmem_limit_bytes=VMEM_LIMIT),
        name="resample",
    )(offs, fracs, cm, rm, hc, after, before, up, dn, lcols, rcols, cup, cdn)


def filter_lanes(tiles, inv, lane):
    n = len(tiles) - 2
    outs = [TAPS[SR] * tiles[j + 1] for j in range(n)]
    for k in range(1, SR + 1):
        fwd = [pltpu.roll(t, LANES - k, 1) for t in tiles[1:]]
        bwd = [pltpu.roll(t, k, 1) for t in tiles[:-1]]
        mf = lane < LANES - k
        mb = lane >= k
        for j in range(n):
            ahead = jnp.where(mf, fwd[j], fwd[j + 1])
            behind = jnp.where(mb, bwd[j + 1], bwd[j])
            outs[j] = outs[j] + TAPS[SR + k] * (ahead + behind)
    return [outs[j] * inv[j] for j in range(n)]


def side_tiles(strip_l, strip_r):
    rows = strip_l.shape[1]
    zero = jnp.zeros((LANES - EDGE, rows), jnp.float32)
    return (
        jnp.concatenate([zero, strip_l], axis=0).T,
        jnp.concatenate([strip_r, zero], axis=0).T,
    )


def fill_sides(scr, s, strip_l, strip_r):
    a, b = side_tiles(strip_l, strip_r)
    scr[0] = a
    scr[1] = b


def across_rows(load, sides, p0, n, inv_ref):
    width = inv_ref.shape[1] // LANES - 2
    lane = lane_iota(n)
    zero = jnp.zeros((n, LANES), jnp.float32)
    tiles = [zero, sides[0, pl.ds(p0, n), :]]
    tiles += [load(p0, n, j) for j in range(width)]
    tiles += [sides[1, pl.ds(p0, n), :], zero]
    inv = [inv_ref[0:1, j * LANES : (j + 1) * LANES] for j in range(width + 2)]
    return filter_lanes(tiles, inv, lane)


def strips_kernel(y_ref, hr_ref, top_ref, bot_ref, lref, rref, inv_ref, z_ref, ftop, fbot, sides):
    scans = top_ref.shape[0]
    rows = lref.shape[2]
    for s in range(scans):
        p = y_ref[0, s]
        for t in range(1, y_ref.shape[0]):
            p = p + y_ref[t, s]
        for t in range(z_ref.shape[0]):
            ext = p.shape[0]
            z_ref[t, s] = jnp.dot(
                hr_ref[t * ext : (t + 1) * ext, :], p,
                precision=HIGHEST, preferred_element_type=jnp.float32,
            )
        fill_sides(sides, s, lref[s], rref[s])

        def load_top(p0, n, j):
            return top_ref[s, :, j * LANES : (j + 1) * LANES]

        def load_bot(p0, n, j):
            return bot_ref[s, :, j * LANES : (j + 1) * LANES]

        for j, v in enumerate(across_rows(load_top, sides, 0, EDGE, inv_ref)):
            ftop[s, j] = v
        for j, v in enumerate(across_rows(load_bot, sides, rows - EDGE, EDGE, inv_ref)):
            fbot[s, j] = v


def strips(y, hr, diff, lstrip, rstrip, inv):
    scans, rows, cols = diff.shape
    ext = y.shape[2]
    n_row = hr.shape[0] // ext
    wide = inv.shape[1]
    return pl.pallas_call(
        strips_kernel,
        grid=(1,),
        in_specs=[
            pl.BlockSpec(y.shape, lambda i: (0, 0, 0, 0)),
            pl.BlockSpec(hr.shape, lambda i: (0, 0)),
            pl.BlockSpec((scans, EDGE, cols), lambda i: (0, 0, 0)),
            pl.BlockSpec((scans, EDGE, cols), lambda i: (0, rows // EDGE - 1, 0)),
            pl.BlockSpec(lstrip.shape, lambda i: (0, 0, 0)),
            pl.BlockSpec(rstrip.shape, lambda i: (0, 0, 0)),
            pl.BlockSpec(inv.shape, lambda i: (0, 0)),
        ],
        out_specs=[
            pl.BlockSpec((n_row, scans, ext, LANES), lambda i: (0, 0, 0, 0)),
            pl.BlockSpec((scans, wide // LANES, EDGE, LANES), lambda i: (0, 0, 0, 0)),
            pl.BlockSpec((scans, wide // LANES, EDGE, LANES), lambda i: (0, 0, 0, 0)),
        ],
        out_shape=[
            jax.ShapeDtypeStruct((n_row, scans, ext, LANES), jnp.float32),
            jax.ShapeDtypeStruct((scans, wide // LANES, EDGE, LANES), jnp.float32),
            jax.ShapeDtypeStruct((scans, wide // LANES, EDGE, LANES), jnp.float32),
        ],
        scratch_shapes=[pltpu.VMEM((2, rows, LANES), jnp.float32)],
        compiler_params=pltpu.CompilerParams(vmem_limit_bytes=VMEM_LIMIT),
        name="strips",
    )(y, hr, diff, diff, lstrip, rstrip, inv)


def final_kernel(
    diff_ref, lref, rref, upr, dnr, z_ref, uc_ref, inv_ref, invr_ref, mc_ref, mr_ref,
    band_ref, slope_ref, sum_ref,
    sides, ac, cu, bd,
):
    rows, cols = diff_ref.shape[1], diff_ref.shape[2]
    wide = inv_ref.shape[1]
    n_out = cols // LANES
    w = z_ref[0, 0]
    for t in range(1, z_ref.shape[0]):
        w = w + z_ref[t, 0]
    n_wide = wide // LANES
    for j in range(n_wide):
        cu[j] = jnp.dot(
            w, uc_ref[:, j * LANES : (j + 1) * LANES],
            precision=HIGHEST, preferred_element_type=jnp.float32,
        )
    fill_sides(sides, 0, lref[0], rref[0])
    for j in range(n_wide):
        ac[j, EDGE : 2 * EDGE, :] = upr[0, j]
        ac[j, 2 * EDGE + rows : 3 * EDGE + rows, :] = dnr[0, j]

    def load(p0, n, j):
        return diff_ref[0, pl.ds(p0, n), j * LANES : (j + 1) * LANES]

    def along_lanes(i, carry):
        p0 = pl.multiple_of(i * 16, 16)
        for j, v in enumerate(across_rows(load, sides, p0, 16, inv_ref)):
            ac[j, pl.ds(p0 + 2 * EDGE, 16), :] = v
        return carry

    lax.fori_loop(0, rows // 16, along_lanes, 0)

    sub = lax.broadcasted_iota(jnp.int32, (8, LANES), 0).astype(jnp.float32)
    f_even = (2.0 * sub + 17.0) * (1.0 / 32.0)
    f_odd = (2.0 * sub + 1.0) * (1.0 / 32.0)

    def band_chunk(c, carry):
        base = pl.multiple_of(c * 8, 8)
        e = lax.div(c, 2)
        f = jnp.where(lax.rem(c, 2) == 1, f_even, f_odd)
        inv = invr_ref[pl.ds(base, 8), :]
        for j in range(n_wide):
            acc = TAPS[SR] * ac[j, pl.ds(base + EDGE, 8), :]
            for k in range(1, SR + 1):
                acc = acc + TAPS[SR + k] * (
                    ac[j, pl.ds(base + EDGE - k, 8), :] + ac[j, pl.ds(base + EDGE + k, 8), :]
                )
            a = cu[j, pl.ds(e, 1), :]
            b = cu[j, pl.ds(e + 1, 1), :]
            bd[j, pl.ds(base, 8), :] = acc * inv - (a + f * (b - a))
        return carry

    lax.fori_loop(0, rows // 8 + 2, band_chunk, 0)

    lane = lane_iota(8)
    first = lane >= 1
    last = lane < LANES - 1

    def slope_chunk(c, carry):
        s1, s2 = carry
        base = pl.multiple_of(c * 8, 8)
        here = [bd[j, pl.ds(base + 8, 8), :] for j in range(n_out + 2)]
        fwd = [pltpu.roll(t, LANES - 1, 1) for t in here[1:]]
        bwd = [pltpu.roll(t, 1, 1) for t in here[:-1]]
        mr = mr_ref[pl.ds(base, 8), :]
        for j in range(n_out):
            so = slice(j * LANES, (j + 1) * LANES)
            gc = jnp.where(last, fwd[j], fwd[j + 1]) - jnp.where(first, bwd[j + 1], bwd[j])
            gc = gc * mc_ref[0:1, so]
            gr = (bd[j + 1, pl.ds(base + 9, 8), :] - bd[j + 1, pl.ds(base + 7, 8), :]) * mr
            sq = gc * gc + gr * gr
            v = here[j + 1]
            band_ref[0, pl.ds(base, 8), so] = v
            slope_ref[0, pl.ds(base, 8), so] = sq
            s1 = s1 + v * v
            s2 = s2 + sq
        return s1, s2

    zero = jnp.zeros((8, LANES), jnp.float32)
    s1, s2 = lax.fori_loop(0, rows // 8, slope_chunk, (zero, zero))
    sum_ref[0, 0:1, :] = jnp.sum(s1, axis=0, keepdims=True)
    sum_ref[0, 1:2, :] = jnp.sum(s2, axis=0, keepdims=True)


def final(diff, lstrip, rstrip, upr, dnr, z, uc, inv, invr, mc, mr):
    scans, rows, cols = diff.shape
    wide = inv.shape[1]
    n_row, _, ext, _ = z.shape
    const2 = lambda s: (0, 0)
    one = lambda s: (s, 0, 0)
    return pl.pallas_call(
        final_kernel,
        grid=(scans,),
        in_specs=[
            pl.BlockSpec((1, rows, cols), one),
            pl.BlockSpec((1, EDGE, rows), one),
            pl.BlockSpec((1, EDGE, rows), one),
            pl.BlockSpec((1, wide // LANES, EDGE, LANES), lambda s: (s, 0, 0, 0)),
            pl.BlockSpec((1, wide // LANES, EDGE, LANES), lambda s: (s, 0, 0, 0)),
            pl.BlockSpec((n_row, 1, ext, LANES), lambda s: (0, s, 0, 0)),
            pl.BlockSpec(uc.shape, const2),
            pl.BlockSpec(inv.shape, const2),
            pl.BlockSpec(invr.shape, const2),
            pl.BlockSpec(mc.shape, const2),
            pl.BlockSpec(mr.shape, const2),
        ],
        out_specs=[
            pl.BlockSpec((1, rows, cols), one),
            pl.BlockSpec((1, rows, cols), one),
            pl.BlockSpec((1, 2, LANES), one),
        ],
        out_shape=[
            jax.ShapeDtypeStruct((scans, rows, cols), jnp.float32),
            jax.ShapeDtypeStruct((scans, rows, cols), jnp.float32),
            jax.ShapeDtypeStruct((scans, 2, LANES), jnp.float32),
        ],
        scratch_shapes=[
            pltpu.VMEM((2, rows, LANES), jnp.float32),
            pltpu.VMEM((wide // LANES, rows + 4 * EDGE, LANES), jnp.float32),
            pltpu.VMEM((wide // LANES, ext, LANES), jnp.float32),
            pltpu.VMEM((wide // LANES, rows + 2 * EDGE, LANES), jnp.float32),
        ],
        compiler_params=pltpu.CompilerParams(vmem_limit_bytes=VMEM_LIMIT),
        name="final",
    )(diff, lstrip, rstrip, upr, dnr, z, uc, inv, invr, mc, mr)


def window_weight(index, count):
    total = jnp.zeros(index.shape, jnp.float32)
    for k in range(-SR, SR + 1):
        inside = (index + k >= 0) & (index + k < count)
        total = total + jnp.where(inside, TAPS[k + SR], 0.0)
    return total


def mean_matrix(start, length, count, width):
    fine = start + lax.broadcasted_iota(jnp.int32, (length, 1), 0)
    blocks = start // BLOCK - 1 + lax.broadcasted_iota(jnp.int32, (1, width), 1)
    valid = lax.broadcasted_iota(jnp.int32, (1, width), 1) < length // BLOCK + 2
    total = jnp.zeros((length, width), jnp.float32)
    for k in range(-SR, SR + 1):
        other = fine + k
        inside = (other >= 0) & (other < count)
        coef = jnp.where(inside, TAPS[k + SR] / (BLOCK * window_weight(other, count)), 0.0)
        total = total + jnp.where((other // BLOCK == blocks) & valid, coef, 0.0)
    return total


def gauss(distance):
    scaled = (distance * BLOCK).astype(jnp.float32) / (ALPHA * LCUT)
    return jnp.exp(-math.pi * scaled * scaled)


def long_matrix(start_block, per_tile, tiles, ext, axis_first):
    count = per_tile * tiles
    src = start_block - 1 + jnp.arange(ext, dtype=jnp.int32)
    src_ok = jnp.arange(ext) < per_tile + 2
    e = jnp.arange(ext, dtype=jnp.int32)
    tgt = (jnp.arange(tiles, dtype=jnp.int32)[:, None] * per_tile - 1 + e[None, :]).reshape(-1)
    tgt = jnp.clip(tgt, 0, count - 1)
    norm = jnp.sum(gauss(jnp.arange(count, dtype=jnp.int32)[:, None] - tgt[None, :]), axis=0)
    m = gauss(src[:, None] - tgt[None, :]) / norm[None, :]
    m = jnp.where(src_ok[:, None], m, 0.0)
    return m if axis_first else m.T


def upsample_cols(per_tile, wide):
    q = lax.broadcasted_iota(jnp.int32, (LANES, wide), 1) - LANES
    num = 2 * q + 1 - BLOCK
    low = num // (2 * BLOCK)
    frac = (num - low * (2 * BLOCK)).astype(jnp.float32) / (2.0 * BLOCK)
    e = lax.broadcasted_iota(jnp.int32, (LANES, wide), 0)
    near = (q >= -1) & (q <= per_tile * BLOCK)
    m = jnp.where(e == low + 1, 1.0 - frac, 0.0) + jnp.where(e == low + 2, frac, 0.0)
    return jnp.where(near, m, 0.0)


def gather_sum_ready(y, axis):
    return lax.all_to_all(y, axis, 0, 0, tiled=True)


def body(before_scan, after_scan, drift_offsets, drift_fractions):
    scans, rows, cols = before_scan.shape
    n_row, n_col = lax.axis_size("row"), lax.axis_size("col")
    row, col = lax.axis_index("row"), lax.axis_index("col")
    offs = drift_offsets.reshape(2, scans)
    fracs = drift_fractions.reshape(2, scans)
    row_down = [(i, i + 1) for i in range(n_row - 1)]
    row_up = [(j, i) for i, j in row_down]
    col_down = [(i, i + 1) for i in range(n_col - 1)]
    col_up = [(j, i) for i, j in col_down]

    top, bot, left, right = pack(after_scan, offs)
    up = lax.ppermute(bot, "row", row_down)
    dn = lax.ppermute(top, "row", row_up)
    lcols = lax.ppermute(right, "col", col_down)
    rcols = lax.ppermute(left, "col", col_up)

    slot = lax.broadcasted_iota(jnp.int32, lcols.shape, 1).astype(jnp.float32)
    for_up = jnp.where(slot < up[:, 0, 0:1, 0:1] + 2.0, rcols, lcols)
    for_dn = jnp.where(slot < dn[:, 0, HALO - 1 : HALO, 0:1] + 2.0, rcols, lcols)
    cup = lax.ppermute(for_dn, "row", row_down)
    cdn = lax.ppermute(for_up, "row", row_up)

    wide = cols + 2 * LANES
    ext = 24
    cm = mean_matrix(col * cols, cols, n_col * cols, LANES)
    rm = mean_matrix(row * rows, rows, n_row * rows, ext).T
    hc = long_matrix(col * (cols // BLOCK), cols // BLOCK, n_col, LANES, True)
    hr = long_matrix(row * (rows // BLOCK), rows // BLOCK, n_row, ext, False)
    uc = upsample_cols(cols // BLOCK, wide)
    qg = col * cols - LANES + jnp.arange(wide, dtype=jnp.int32)
    near = (qg >= col * cols - 1) & (qg <= (col + 1) * cols)
    inv = jnp.where(near, 1.0 / jnp.where(near, window_weight(qg, n_col * cols), 1.0), 0.0)[None, :]
    pg = row * rows - EDGE + jnp.arange(rows + 2 * EDGE, dtype=jnp.int32)
    nearr = (pg >= row * rows - 1) & (pg <= (row + 1) * rows)
    invr = jnp.where(nearr, 1.0 / jnp.where(nearr, window_weight(pg, n_row * rows), 1.0), 0.0)
    invr = jnp.broadcast_to(invr[:, None], (rows + 2 * EDGE, LANES))
    qi = col * cols + jnp.arange(cols, dtype=jnp.int32)
    mc = ((qi >= 1) & (qi <= n_col * cols - 2)).astype(jnp.float32)[None, :]
    pi = row * rows + jnp.arange(rows, dtype=jnp.int32)
    mr = ((pi >= 1) & (pi <= n_row * rows - 2)).astype(jnp.float32)
    mr = jnp.broadcast_to(mr[:, None], (rows, LANES))

    diff, edge_l, edge_r, y = resample(
        offs, fracs, cm, rm, hc, after_scan, before_scan, up, dn, lcols, rcols, cup, cdn
    )
    lstrip = lax.ppermute(edge_r, "col", col_down)
    rstrip = lax.ppermute(edge_l, "col", col_up)
    y = lax.all_to_all(y, "col", 0, 0, tiled=True)
    z, ftop, fbot = strips(y, hr, diff, lstrip, rstrip, inv)
    upr = lax.ppermute(fbot, "row", row_down)
    dnr = lax.ppermute(ftop, "row", row_up)
    z = lax.all_to_all(z, "row", 0, 0, tiled=True)
    band, slope, sums = final(diff, lstrip, rstrip, upr, dnr, z, uc, inv, invr, mc, mr)

    mine = jnp.sum(sums, axis=2).T.reshape(1, 2 * scans)
    mine = jnp.broadcast_to(mine[:, None, :], (n_row * n_col, 1, 2 * scans))
    every = lax.all_to_all(mine, ("row", "col"), 0, 0, tiled=True)
    total = jnp.sum(every, axis=(0, 1)).reshape(2, scans)
    cells = n_row * rows * n_col * cols
    return band, slope, jnp.sqrt(total / cells + EPSILON)


def solution(mesh):
    in_specs = (
        P(None, "row", "col"),
        P(None, "row", "col"),
        P(None, None, "row", "col"),
        P(None, None, "row", "col"),
    )
    out_specs = (P(None, "row", "col"), P(None, "row", "col"), P())
    return jax.shard_map(body, mesh=mesh, in_specs=in_specs, out_specs=out_specs, check_vma=False)
```

```python
import math

import jax
import jax.numpy as jnp
from jax import lax
from jax.experimental import pallas as pl
from jax.experimental.pallas import tpu as pltpu
from jax.sharding import PartitionSpec as P

LS = 5
SR = 4
LCUT = 1600
BLOCK = 16
ALPHA = math.sqrt(math.log(2.0) / math.pi)
EPSILON = 1e-06
HIGHEST = lax.Precision.HIGHEST
HALO = 136
EDGE = 8
LANES = 128
TAPS = [math.exp(-math.pi * (k / (ALPHA * LS)) ** 2) for k in range(-SR, SR + 1)]
VMEM_LIMIT = 56 * 1024 * 1024


def lane_iota(rows):
    return lax.broadcasted_iota(jnp.int32, (rows, LANES), 1)


def pack_kernel(offs_ref, x_ref, top_ref, bot_ref, left_ref, right_ref):
    s = pl.program_id(0)
    shift = offs_ref[1, s].astype(jnp.float32)
    rows, cols = x_ref.shape[1], x_ref.shape[2]
    for j in range(cols // LANES):
        sl = slice(j * LANES, (j + 1) * LANES)
        top_ref[0, j] = x_ref[0, 0:HALO, sl]
        bot_ref[0, j] = x_ref[0, rows - HALO : rows, sl]
    top_ref[0, 0, HALO - 1 : HALO, :] = jnp.full((1, LANES), shift, jnp.float32)
    bot_ref[0, 0, 0:1, :] = jnp.full((1, LANES), shift, jnp.float32)
    left_ref[0] = x_ref[0, :, 0:256].T[0:HALO, :]
    right_ref[0] = x_ref[0, :, cols - 256 : cols].T[256 - HALO : 256, :]


def pack(after, offs):
    scans, rows, cols = after.shape
    n_tiles = cols // LANES
    return pl.pallas_call(
        pack_kernel,
        grid=(scans,),
        in_specs=[
            pl.BlockSpec(memory_space=pltpu.SMEM),
            pl.BlockSpec((1, rows, cols), lambda s: (s, 0, 0)),
        ],
        out_specs=[
            pl.BlockSpec((1, n_tiles, HALO, LANES), lambda s: (s, 0, 0, 0)),
            pl.BlockSpec((1, n_tiles, HALO, LANES), lambda s: (s, 0, 0, 0)),
            pl.BlockSpec((1, HALO, rows), lambda s: (s, 0, 0)),
            pl.BlockSpec((1, HALO, rows), lambda s: (s, 0, 0)),
        ],
        out_shape=[
            jax.ShapeDtypeStruct((scans, n_tiles, HALO, LANES), jnp.float32),
            jax.ShapeDtypeStruct((scans, n_tiles, HALO, LANES), jnp.float32),
            jax.ShapeDtypeStruct((scans, HALO, rows), jnp.float32),
            jax.ShapeDtypeStruct((scans, HALO, rows), jnp.float32),
        ],
        name="pack",
    )(offs, after)


def flip_kernel(x_ref, o_ref):
    rows, cols = x_ref.shape[1], x_ref.shape[2]
    for j in range(cols // LANES):
        for h in range(rows // LANES):
            block = x_ref[0, h * LANES : (h + 1) * LANES, j * LANES : (j + 1) * LANES]
            o_ref[0, h, j * LANES : (j + 1) * LANES, :] = block.T


def flip(x):
    scans, rows, cols = x.shape
    halves = rows // LANES
    return pl.pallas_call(
        flip_kernel,
        grid=(scans,),
        in_specs=[pl.BlockSpec((1, rows, cols), lambda s: (s, 0, 0))],
        out_specs=pl.BlockSpec((1, halves, cols, LANES), lambda s: (s, 0, 0, 0)),
        out_shape=jax.ShapeDtypeStruct((scans, halves, cols, LANES), jnp.float32),
        cost_estimate=pl.CostEstimate(
            flops=x.size, bytes_accessed=8 * x.size, transcendentals=0
        ),
        name="flip",
    )(x)


def scalar_taps(fraction):
    t = fraction.astype(jnp.float32) * (1.0 / 256.0)
    t2 = t * t
    t3 = t2 * t
    return (
        0.5 * (2.0 * t2 - t3 - t),
        0.5 * (3.0 * t3 - 5.0 * t2 + 2.0),
        0.5 * (4.0 * t2 - 3.0 * t3 + t),
        0.5 * (t3 - t2),
    )


CB = 64


def resample_kernel(
    offs_ref, fracs_ref, wt_ref, rm_ref, hc_ref,
    after, beforet, up, dn, lcols, rcols, cup, cdn,
    diff_out, edge_l, edge_r, y_ref,
    win, stage, bef, dif, rowsum, sums, part, sem, bsem, osem,
):
    scans, n_tiles = win.shape[0], win.shape[1]
    halves, cols = bef.shape[1], bef.shape[2]
    rows = halves * LANES
    n_out = cols // LANES
    left = 2 * LANES

    def copies(s):
        return [
            (after.at[s, :, pl.ds(j * LANES, LANES)], win.at[s, 2 + j, pl.ds(HALO, rows), :])
            for j in range(n_out)
        ] + [
            (up.at[s], win.at[s, pl.ds(2, n_out), pl.ds(0, HALO), :]),
            (dn.at[s], win.at[s, pl.ds(2, n_out), pl.ds(HALO + rows, HALO), :]),
            (lcols.at[s], stage.at[s, 0, pl.ds(256 - HALO, HALO), :]),
            (rcols.at[s], stage.at[s, 1, pl.ds(0, HALO), :]),
            (cup.at[s], stage.at[s, 2, pl.ds(256 - HALO, HALO), :]),
            (cup.at[s], stage.at[s, 3, pl.ds(0, HALO), :]),
            (cdn.at[s], stage.at[s, 4, pl.ds(256 - HALO, HALO), :]),
            (cdn.at[s], stage.at[s, 5, pl.ds(0, HALO), :]),
        ]

    for s in range(scans):
        for n, (a, b) in enumerate(copies(s)):
            pltpu.make_async_copy(a, b, sem.at[s, n]).start()
        pltpu.make_async_copy(beforet.at[s], bef.at[s], bsem.at[s]).start()
    part[...] = jnp.zeros_like(part)
    sums[...] = jnp.zeros_like(sums)
    n_blocks = cols // BLOCK
    weight = [wt_ref[8 * i : 8 * i + 8, :] for i in range(8)]

    def one_scan(s, carry):
        for n, (a, b) in enumerate(copies(s)):
            pltpu.make_async_copy(a, b, sem.at[s, n]).wait()
        pltpu.make_async_copy(beforet.at[s], bef.at[s], bsem.at[s]).wait()
        dr = offs_ref[0, s]
        dc = offs_ref[1, s]

        def put(slot, first_tile, row0, cut):
            flipped = stage[s, slot].T
            for h in range(2):
                win[s, first_tile + h, row0 : row0 + cut.stop - cut.start, :] = flipped[
                    cut, h * LANES : (h + 1) * LANES
                ]

        def put_side(first_tile, slots):
            put(slots[0], first_tile, HALO, slice(0, rows))

            @pl.when(dr <= 0)
            def _():
                put(slots[1], first_tile, 0, slice(rows - HALO, rows))

            @pl.when(dr >= -1)
            def _():
                put(slots[2], first_tile, HALO + rows, slice(0, HALO))

        @pl.when(dc <= 0)
        def _():
            put_side(0, (0, 2, 4))

        @pl.when(dc >= -1)
        def _():
            put_side(2 + n_out, (1, 3, 5))

        rt = scalar_taps(fracs_ref[0, s])
        ct = scalar_taps(fracs_ref[1, s])
        r0 = HALO + dr - 1
        c0 = left + dc - 1
        k = lax.div(c0, LANES)
        r = c0 - k * LANES

        def row_taps(i, carry):
            outs = []
            for j in range(2):
                for h in range(halves):
                    first = r0 + h * LANES
                    acc = rt[0] * win[s, k + 2 * i + j, pl.ds(first, LANES), :]
                    for a in range(1, 4):
                        acc = acc + rt[a] * win[s, k + 2 * i + j, pl.ds(first + a, LANES), :]
                    outs.append(acc.T)
            for j in range(2):
                for h in range(halves):
                    at = pl.multiple_of((2 * i + j) * LANES, LANES)
                    rowsum[h, pl.ds(at, LANES), :] = outs[j * halves + h]
            return carry

        lax.fori_loop(0, (n_out + 2) // 2, row_taps, 0)

        def col_taps(i, carry):
            q0 = pl.multiple_of(i * CB, CB)
            for h in range(halves):
                acc = ct[0] * rowsum[h, pl.ds(r + q0, CB), :]
                for b in range(1, 4):
                    acc = acc + ct[b] * rowsum[h, pl.ds(r + q0 + b, CB), :]
                dif[s, h, pl.ds(q0, CB), :] = bef[s, h, pl.ds(q0, CB), :] - acc
            return carry

        lax.fori_loop(0, cols // CB, col_taps, 0)
        pltpu.make_async_copy(dif.at[s], diff_out.at[s], osem.at[s]).start()
        for h in range(halves):
            edge_l[s, h] = dif[s, h, 0:EDGE, :]
            edge_r[s, h] = dif[s, h, cols - EDGE : cols, :]

        def block_sums(i, carry):
            for h in range(halves):
                total = []
                for e in range(8):
                    q = pl.multiple_of(i * LANES + e * BLOCK, BLOCK)
                    qa = pl.multiple_of(jnp.maximum(q - 8, 0), 8)
                    qb = pl.multiple_of(jnp.minimum(q + 16, cols - 8), 8)
                    t = weight[0] * dif[s, h, pl.ds(qa, 8), :]
                    t = t + weight[1] * dif[s, h, pl.ds(q, 8), :]
                    t = t + weight[2] * dif[s, h, pl.ds(q + 8, 8), :]
                    t = t + weight[3] * dif[s, h, pl.ds(qb, 8), :]
                    total.append(jnp.sum(t, axis=0, keepdims=True))
                at = pl.multiple_of(i * 8 + 8, 8)
                sums[pl.ds(at, 8), h * LANES : (h + 1) * LANES] = jnp.concatenate(total, axis=0)
            return carry

        lax.fori_loop(0, n_blocks // 8, block_sums, 0)
        for h in range(halves):
            sl = slice(h * LANES, (h + 1) * LANES)
            v = [dif[s, h, 8 * i : 8 * i + 8, :] for i in range(3)]
            w = [dif[s, h, cols - 24 + 8 * i : cols - 16 + 8 * i, :] for i in range(3)]
            rows_at = (
                (7, weight[4] * v[0]),
                (8, weight[5] * v[0] + weight[2] * v[1] + weight[3] * v[2]),
                (7 + n_blocks, weight[0] * w[0] + weight[1] * w[1] + weight[6] * w[2]),
                (8 + n_blocks, weight[7] * w[2]),
            )
            for at, t in rows_at:
                sums[at : at + 1, sl] = jnp.sum(t, axis=0, keepdims=True)
        part[...] += jnp.dot(
            sums[...], rm_ref[s], precision=HIGHEST, preferred_element_type=jnp.float32
        )
        return carry

    lax.fori_loop(0, scans, one_scan, 0)
    y = jnp.dot(hc_ref[...], part[...], precision=HIGHEST, preferred_element_type=jnp.float32)
    ext = hc_ref.shape[0] // y_ref.shape[0]
    for t in range(y_ref.shape[0]):
        y_ref[t] = y[t * ext : (t + 1) * ext, :]
    for s in range(scans):
        pltpu.make_async_copy(dif.at[s], diff_out.at[s], osem.at[s]).wait()


def resample(offs, fracs, wt, rm, hc, ext, after, beforet, up, dn, lcols, rcols, cup, cdn):
    scans, rows, cols = after.shape
    halves = rows // LANES
    n_col = hc.shape[0] // ext
    anywhere = pl.BlockSpec(memory_space=pl.ANY)
    vmem = pl.BlockSpec(memory_space=pltpu.VMEM)
    smem = pl.BlockSpec(memory_space=pltpu.SMEM)
    return pl.pallas_call(
        resample_kernel,
        in_specs=[smem, smem, vmem, vmem, vmem] + [anywhere] * 8,
        out_specs=[anywhere, vmem, vmem, vmem],
        out_shape=[
            jax.ShapeDtypeStruct((scans, halves, cols, LANES), jnp.float32),
            jax.ShapeDtypeStruct((scans, halves, EDGE, LANES), jnp.float32),
            jax.ShapeDtypeStruct((scans, halves, EDGE, LANES), jnp.float32),
            jax.ShapeDtypeStruct((n_col, ext, LANES), jnp.float32),
        ],
        scratch_shapes=[
            pltpu.VMEM((scans, cols // LANES + 4, 2 * HALO + rows, LANES), jnp.float32),
            pltpu.VMEM((scans, 6, 256, rows), jnp.float32),
            pltpu.VMEM((scans, halves, cols, LANES), jnp.float32),
            pltpu.VMEM((scans, halves, cols, LANES), jnp.float32),
            pltpu.VMEM((halves, cols + 2 * LANES, LANES), jnp.float32),
            pltpu.VMEM((hc.shape[1], rows), jnp.float32),
            pltpu.VMEM((hc.shape[1], LANES), jnp.float32),
            pltpu.SemaphoreType.DMA((scans, cols // LANES + 8)),
            pltpu.SemaphoreType.DMA((scans,)),
            pltpu.SemaphoreType.DMA((scans,)),
        ],
        compiler_params=pltpu.CompilerParams(vmem_limit_bytes=VMEM_LIMIT),
        name="resample",
    )(offs, fracs, wt, rm, hc, after, beforet, up, dn, lcols, rcols, cup, cdn)


def long_rows_kernel(y_ref, hr_ref, z_ref):
    n_row, scans, ext, _ = z_ref.shape
    p = y_ref[0]
    for t in range(1, y_ref.shape[0]):
        p = p + y_ref[t]
    p = jnp.concatenate([p, jnp.zeros((LANES - p.shape[0], LANES), jnp.float32)], axis=0).T
    for s in range(scans):
        z = jnp.dot(
            hr_ref[...], p[s * ext : (s + 1) * ext, :],
            precision=HIGHEST, preferred_element_type=jnp.float32,
        )
        for t in range(n_row):
            z_ref[t, s] = z[t * ext : (t + 1) * ext, :]


def long_rows(y, hr, scans):
    ext = hr.shape[1]
    vmem = pl.BlockSpec(memory_space=pltpu.VMEM)
    return pl.pallas_call(
        long_rows_kernel,
        in_specs=[vmem, vmem],
        out_specs=vmem,
        out_shape=jax.ShapeDtypeStruct((hr.shape[0] // ext, scans, ext, LANES), jnp.float32),
        name="long_rows",
    )(y, hr)


PAD = 2 * EDGE


def across_kernel(invc_ref, diff, lstrip, rstrip, ac_out, ftop, fbot, buf, acs, sem, osem):
    scans, halves, cols = diff.shape[0], diff.shape[1], diff.shape[2]
    n_out = cols // LANES
    rows = halves * LANES

    def copies(s):
        return [
            (diff.at[s], buf.at[s, :, pl.ds(PAD, cols), :]),
            (lstrip.at[s], buf.at[s, :, pl.ds(PAD - EDGE, EDGE), :]),
            (rstrip.at[s], buf.at[s, :, pl.ds(PAD + cols, EDGE), :]),
        ]

    for s in range(scans):
        for n, (a, b) in enumerate(copies(s)):
            pltpu.make_async_copy(a, b, sem.at[s, n]).start()
    zero = jnp.zeros((LANES - EDGE, LANES), jnp.float32)

    def filtered(s, h, q, n):
        acc = TAPS[SR] * buf[s, h, pl.ds(q + PAD, n), :]
        for k in range(1, SR + 1):
            acc = acc + TAPS[SR + k] * (
                buf[s, h, pl.ds(q + PAD - k, n), :] + buf[s, h, pl.ds(q + PAD + k, n), :]
            )
        return acc

    def one_scan(s, carry):
        for n, (a, b) in enumerate(copies(s)):
            pltpu.make_async_copy(a, b, sem.at[s, n]).wait()
        for h in range(halves):
            buf[s, h, 0 : PAD - EDGE, :] = zero[0:EDGE]
            buf[s, h, PAD + cols + EDGE :, :] = zero[0:EDGE]
        for h in range(halves):
            sl = slice(h * LANES, (h + 1) * LANES)
            lo = filtered(s, h, -EDGE, EDGE) * invc_ref[0:EDGE, :]
            hi = filtered(s, h, cols, EDGE) * invc_ref[EDGE + cols : 2 * EDGE + cols, :]
            acs[s, 0, sl, :] = jnp.concatenate([zero, lo], axis=0).T
            acs[s, n_out + 1, sl, :] = jnp.concatenate([hi, zero], axis=0).T

        def block(i, carry):
            q0 = pl.multiple_of(i * LANES, LANES)
            inv = invc_ref[pl.ds(q0 + EDGE, LANES), :]
            outs = [(filtered(s, h, q0, LANES) * inv).T for h in range(halves)]
            for h in range(halves):
                acs[s, i + 1, h * LANES : (h + 1) * LANES, :] = outs[h]
            return carry

        lax.fori_loop(0, n_out, block, 0)
        pltpu.make_async_copy(acs.at[s], ac_out.at[s], osem.at[s]).start()
        for j in range(n_out + 2):
            ftop[s, j] = acs[s, j, 0:EDGE, :]
            fbot[s, j] = acs[s, j, rows - EDGE : rows, :]
        return carry

    lax.fori_loop(0, scans, one_scan, 0)
    for s in range(scans):
        pltpu.make_async_copy(acs.at[s], ac_out.at[s], osem.at[s]).wait()


def across(invc, diff, lstrip, rstrip):
    scans, halves, cols, _ = diff.shape
    rows = halves * LANES
    n_wide = cols // LANES + 2
    anywhere = pl.BlockSpec(memory_space=pl.ANY)
    vmem = pl.BlockSpec(memory_space=pltpu.VMEM)
    return pl.pallas_call(
        across_kernel,
        in_specs=[vmem, anywhere, anywhere, anywhere],
        out_specs=[anywhere, vmem, vmem],
        out_shape=[
            jax.ShapeDtypeStruct((scans, n_wide, rows, LANES), jnp.float32),
            jax.ShapeDtypeStruct((scans, n_wide, EDGE, LANES), jnp.float32),
            jax.ShapeDtypeStruct((scans, n_wide, EDGE, LANES), jnp.float32),
        ],
        scratch_shapes=[
            pltpu.VMEM((scans, halves, cols + 2 * PAD, LANES), jnp.float32),
            pltpu.VMEM((scans, n_wide, rows, LANES), jnp.float32),
            pltpu.SemaphoreType.DMA((scans, 3)),
            pltpu.SemaphoreType.DMA((scans,)),
        ],
        compiler_params=pltpu.CompilerParams(vmem_limit_bytes=VMEM_LIMIT),
        cost_estimate=pl.CostEstimate(
            flops=20 * diff.size, bytes_accessed=8 * diff.size, transcendentals=0
        ),
        name="across",
    )(invc, diff, lstrip, rstrip)


def final_kernel(
    z_ref, uc_ref, invr_ref, mc_ref, mr_ref, across_in, upr, dnr,
    band_ref, slope_ref, sum_ref,
    acs, cu, bd, sem,
):
    s = pl.program_id(0)
    scans, n_wide = acs.shape[0], acs.shape[1]
    rows, cols = band_ref.shape[1], band_ref.shape[2]
    n_out = cols // LANES

    def copies(s):
        return [
            (across_in.at[s], acs.at[s, :, pl.ds(PAD, rows), :]),
            (upr.at[s], acs.at[s, :, pl.ds(PAD - EDGE, EDGE), :]),
            (dnr.at[s], acs.at[s, :, pl.ds(PAD + rows, EDGE), :]),
        ]

    @pl.when(s == 0)
    def _():
        for t in range(scans):
            for n, (a, b) in enumerate(copies(t)):
                pltpu.make_async_copy(a, b, sem.at[t, n]).start()

        parts = []
        for t in range(scans):
            w = z_ref[0, t]
            for n in range(1, z_ref.shape[0]):
                w = w + z_ref[n, t]
            parts.append(w)
        w = jnp.concatenate(parts, axis=0)
        total = None
        for _ in range(3):
            piece = w.astype(jnp.bfloat16)
            w = w - piece.astype(jnp.float32)
            term = jnp.dot(piece, uc_ref[...], preferred_element_type=jnp.float32)
            total = term if total is None else total + term
        ext = cu.shape[2]
        for t in range(scans):
            for j in range(n_wide):
                cu[t, j] = total[t * ext : (t + 1) * ext, j * LANES : (j + 1) * LANES]

    for n, (a, b) in enumerate(copies(s)):
        pltpu.make_async_copy(a, b, sem.at[s, n]).wait()
    for j in range(n_wide):
        acs[s, j, 0 : PAD - EDGE, :] = jnp.zeros((PAD - EDGE, LANES), jnp.float32)
        acs[s, j, PAD + rows + EDGE :, :] = jnp.zeros((PAD - EDGE, LANES), jnp.float32)

    sub = lax.broadcasted_iota(jnp.int32, (BLOCK, LANES), 0).astype(jnp.float32)
    f = (2.0 * sub + 1.0) * (1.0 / 32.0)

    def band_rows(e, carry):
        base = pl.multiple_of(e * BLOCK, BLOCK)
        inv = invr_ref[pl.ds(base, BLOCK), :]
        for j in range(n_wide):
            acc = TAPS[SR] * acs[s, j, pl.ds(base + EDGE, BLOCK), :]
            for k in range(1, SR + 1):
                acc = acc + TAPS[SR + k] * (
                    acs[s, j, pl.ds(base + EDGE - k, BLOCK), :]
                    + acs[s, j, pl.ds(base + EDGE + k, BLOCK), :]
                )
            a = cu[s, j, pl.ds(e, 1), :]
            b = cu[s, j, pl.ds(e + 1, 1), :]
            bd[j, pl.ds(base, BLOCK), :] = acc * inv - (a + f * (b - a))
        return carry

    lax.fori_loop(0, rows // BLOCK + 1, band_rows, 0)

    lane = lane_iota(BLOCK)
    first = lane >= 1
    last = lane < LANES - 1

    def slope_rows(c, carry):
        s1, s2 = carry
        base = pl.multiple_of(c * BLOCK, BLOCK)
        here = [bd[j, pl.ds(base + EDGE, BLOCK), :] for j in range(n_wide)]
        fwd = [pltpu.roll(t, LANES - 1, 1) for t in here[1:]]
        bwd = [pltpu.roll(t, 1, 1) for t in here[:-1]]
        mr = mr_ref[pl.ds(base, BLOCK), :]
        for j in range(n_out):
            so = slice(j * LANES, (j + 1) * LANES)
            gc = jnp.where(last, fwd[j], fwd[j + 1]) - jnp.where(first, bwd[j + 1], bwd[j])
            gc = gc * mc_ref[0:1, so]
            gr = (
                bd[j + 1, pl.ds(base + EDGE + 1, BLOCK), :]
                - bd[j + 1, pl.ds(base + EDGE - 1, BLOCK), :]
            ) * mr
            sq = gc * gc + gr * gr
            v = here[j + 1]
            band_ref[0, pl.ds(base, BLOCK), so] = v
            slope_ref[0, pl.ds(base, BLOCK), so] = sq
            s1 = s1 + v * v
            s2 = s2 + sq
        return s1, s2

    zero = jnp.zeros((BLOCK, LANES), jnp.float32)
    s1, s2 = lax.fori_loop(0, rows // BLOCK, slope_rows, (zero, zero))
    sum_ref[0, 0:1, :] = jnp.sum(s1, axis=0, keepdims=True)
    sum_ref[0, 1:2, :] = jnp.sum(s2, axis=0, keepdims=True)


def final(z, uc, invr, mc, mr, ac, upr, dnr):
    scans, n_wide, rows, _ = ac.shape
    cols = mc.shape[1]
    n_row, _, ext, _ = z.shape
    const2 = lambda s: (0, 0)
    one = lambda s: (s, 0, 0)
    anywhere = pl.BlockSpec(memory_space=pl.ANY)
    return pl.pallas_call(
        final_kernel,
        grid=(scans,),
        in_specs=[
            pl.BlockSpec(z.shape, lambda s: (0, 0, 0, 0)),
            pl.BlockSpec(uc.shape, const2),
            pl.BlockSpec(invr.shape, const2),
            pl.BlockSpec(mc.shape, const2),
            pl.BlockSpec(mr.shape, const2),
            anywhere,
            anywhere,
            anywhere,
        ],
        out_specs=[
            pl.BlockSpec((1, rows, cols), one),
            pl.BlockSpec((1, rows, cols), one),
            pl.BlockSpec((1, 2, LANES), one),
        ],
        out_shape=[
            jax.ShapeDtypeStruct((scans, rows, cols), jnp.float32),
            jax.ShapeDtypeStruct((scans, rows, cols), jnp.float32),
            jax.ShapeDtypeStruct((scans, 2, LANES), jnp.float32),
        ],
        scratch_shapes=[
            pltpu.VMEM((scans, n_wide, rows + 2 * PAD, LANES), jnp.float32),
            pltpu.VMEM((scans, n_wide, ext, LANES), jnp.float32),
            pltpu.VMEM((n_wide, rows + 2 * EDGE, LANES), jnp.float32),
            pltpu.SemaphoreType.DMA((scans, 3)),
        ],
        compiler_params=pltpu.CompilerParams(vmem_limit_bytes=VMEM_LIMIT),
        name="final",
    )(z, uc, invr, mc, mr, ac, upr, dnr)


def window_weight(index, count):
    total = jnp.zeros(index.shape, jnp.float32)
    for k in range(-SR, SR + 1):
        inside = (index + k >= 0) & (index + k < count)
        total = total + jnp.where(inside, TAPS[k + SR], 0.0)
    return total


def mean_matrix(start, length, count, width):
    fine = start + lax.broadcasted_iota(jnp.int32, (length, 1), 0)
    blocks = start // BLOCK - 1 + lax.broadcasted_iota(jnp.int32, (1, width), 1)
    valid = lax.broadcasted_iota(jnp.int32, (1, width), 1) < length // BLOCK + 2
    total = jnp.zeros((length, width), jnp.float32)
    for k in range(-SR, SR + 1):
        other = fine + k
        inside = (other >= 0) & (other < count)
        coef = jnp.where(inside, TAPS[k + SR] / (BLOCK * window_weight(other, count)), 0.0)
        total = total + jnp.where((other // BLOCK == blocks) & valid, coef, 0.0)
    return total


def mean_weights(start, length, count):
    b = BLOCK
    cases = (
        (8 * b - 8, 8), (8 * b, 8), (8 * b + 8, 8), (9 * b, 8),
        (0, -1), (0, 0), (length - 8, length // b - 1), (length - 8, length // b),
    )
    base = jnp.array([c[0] for c in cases], jnp.int32)[:, None]
    block = jnp.array([c[1] for c in cases], jnp.int32)[:, None] + start // b
    fine = start + base + jnp.arange(8, dtype=jnp.int32)[None, :]
    total = jnp.zeros(fine.shape, jnp.float32)
    for k in range(-SR, SR + 1):
        other = fine + k
        inside = (other >= 0) & (other < count) & (other // b == block)
        total = total + jnp.where(inside, TAPS[k + SR] / (b * window_weight(other, count)), 0.0)
    return jnp.broadcast_to(total.reshape(64, 1), (64, LANES))


def gauss(distance):
    scaled = (distance * BLOCK).astype(jnp.float32) / (ALPHA * LCUT)
    return jnp.exp(-math.pi * scaled * scaled)


def long_matrix(start_block, per_tile, tiles, src_ext, src_first, ext):
    count = per_tile * tiles
    i = jnp.arange(src_ext, dtype=jnp.int32)
    src = start_block - src_first + i
    src_ok = (i >= src_first - 1) & (i <= src_first + per_tile)
    e = jnp.arange(ext, dtype=jnp.int32)
    tgt = (jnp.arange(tiles, dtype=jnp.int32)[:, None] * per_tile - 1 + e[None, :]).reshape(-1)
    tgt = jnp.clip(tgt, 0, count - 1)
    norm = jnp.sum(gauss(jnp.arange(count, dtype=jnp.int32)[None, :] - tgt[:, None]), axis=1)
    m = gauss(src[None, :] - tgt[:, None]) / norm[:, None]
    return jnp.where(src_ok[None, :], m, 0.0)


def upsample_cols(per_tile, wide):
    q = lax.broadcasted_iota(jnp.int32, (LANES, wide), 1) - LANES
    num = 2 * q + 1 - BLOCK
    low = num // (2 * BLOCK)
    frac = (num - low * (2 * BLOCK)).astype(jnp.float32) / (2.0 * BLOCK)
    e = lax.broadcasted_iota(jnp.int32, (LANES, wide), 0)
    near = (q >= -1) & (q <= per_tile * BLOCK)
    m = jnp.where(e == low + 1, 1.0 - frac, 0.0) + jnp.where(e == low + 2, frac, 0.0)
    return jnp.where(near, m, 0.0).astype(jnp.bfloat16)


def body(before_scan, after_scan, drift_offsets, drift_fractions):
    scans, rows, cols = before_scan.shape
    n_row, n_col = lax.axis_size("row"), lax.axis_size("col")
    row, col = lax.axis_index("row"), lax.axis_index("col")
    offs = drift_offsets.reshape(2, scans)
    fracs = drift_fractions.reshape(2, scans)
    row_down = [(i, i + 1) for i in range(n_row - 1)]
    row_up = [(j, i) for i, j in row_down]
    col_down = [(i, i + 1) for i in range(n_col - 1)]
    col_up = [(j, i) for i, j in col_down]

    top, bot, left, right = pack(after_scan, offs)
    up = lax.ppermute(bot, "row", row_down)
    dn = lax.ppermute(top, "row", row_up)
    lcols = lax.ppermute(right, "col", col_down)
    rcols = lax.ppermute(left, "col", col_up)

    slot = lax.broadcasted_iota(jnp.int32, lcols.shape, 1).astype(jnp.float32)
    for_up = jnp.where(slot < up[:, 0, 0:1, 0:1] + 2.0, rcols, lcols)
    for_dn = jnp.where(slot < dn[:, 0, HALO - 1 : HALO, 0:1] + 2.0, rcols, lcols)
    cup = lax.ppermute(for_dn, "row", row_down)
    cdn = lax.ppermute(for_up, "row", row_up)

    wide = cols + 2 * LANES
    ext_r, ext_c = 24, 72
    wt = mean_weights(col * cols, cols, n_col * cols)
    rm = mean_matrix(row * rows, rows, n_row * rows, ext_r)
    rm = jnp.stack([jnp.pad(rm, ((0, 0), (s * ext_r, LANES - (s + 1) * ext_r))) for s in range(scans)])
    hc = long_matrix(col * (cols // BLOCK), cols // BLOCK, n_col, cols // BLOCK + 16, 8, ext_c)
    hr = long_matrix(row * (rows // BLOCK), rows // BLOCK, n_row, ext_r, 1, ext_r)
    uc = upsample_cols(cols // BLOCK, wide)
    qg = col * cols - EDGE + jnp.arange(cols + 2 * EDGE, dtype=jnp.int32)
    near = (qg >= col * cols - 1) & (qg <= (col + 1) * cols)
    inv = jnp.where(near, 1.0 / jnp.where(near, window_weight(qg, n_col * cols), 1.0), 0.0)
    inv = jnp.broadcast_to(inv[:, None], (cols + 2 * EDGE, LANES))
    pg = row * rows - EDGE + jnp.arange(rows + 2 * EDGE, dtype=jnp.int32)
    nearr = (pg >= row * rows - 1) & (pg <= (row + 1) * rows)
    invr = jnp.where(nearr, 1.0 / jnp.where(nearr, window_weight(pg, n_row * rows), 1.0), 0.0)
    invr = jnp.broadcast_to(invr[:, None], (rows + 2 * EDGE, LANES))
    qi = col * cols + jnp.arange(cols, dtype=jnp.int32)
    mc = ((qi >= 1) & (qi <= n_col * cols - 2)).astype(jnp.float32)[None, :]
    pi = row * rows + jnp.arange(rows, dtype=jnp.int32)
    mr = ((pi >= 1) & (pi <= n_row * rows - 2)).astype(jnp.float32)
    mr = jnp.broadcast_to(mr[:, None], (rows, LANES))

    diff, edge_l, edge_r, y = resample(
        offs, fracs, wt, rm, hc, ext_c, after_scan, flip(before_scan), up, dn, lcols, rcols, cup, cdn
    )
    lstrip = lax.ppermute(edge_r, "col", col_down)
    rstrip = lax.ppermute(edge_l, "col", col_up)
    y = lax.all_to_all(y, "col", 0, 0, tiled=True)
    ac, ftop, fbot = across(inv, diff, lstrip, rstrip)
    y, ac, ftop, fbot = lax.optimization_barrier((y, ac, ftop, fbot))
    z = long_rows(y, hr, scans)
    upr = lax.ppermute(fbot, "row", row_down)
    dnr = lax.ppermute(ftop, "row", row_up)
    z = lax.all_to_all(z, "row", 0, 0, tiled=True)
    band, slope, sums = final(z, uc, invr, mc, mr, ac, upr, dnr)

    mine = jnp.sum(sums, axis=2).T.reshape(1, 2 * scans)
    mine = jnp.broadcast_to(mine[:, None, :], (n_row * n_col, 1, 2 * scans))
    every = lax.all_to_all(mine, ("row", "col"), 0, 0, tiled=True)
    total = jnp.sum(every, axis=(0, 1)).reshape(2, scans)
    cells = n_row * rows * n_col * cols
    return band, slope, jnp.sqrt(total / cells + EPSILON)


def solution(mesh):
    in_specs = (
        P(None, "row", "col"),
        P(None, "row", "col"),
        P(None, None, "row", "col"),
        P(None, None, "row", "col"),
    )
    out_specs = (P(None, "row", "col"), P(None, "row", "col"), P())
    return jax.shard_map(body, mesh=mesh, in_specs=in_specs, out_specs=out_specs, check_vma=False)
```

```python
import math

import jax
import jax.numpy as jnp
from jax import lax
from jax.experimental import pallas as pl
from jax.experimental.pallas import tpu as pltpu
from jax.sharding import PartitionSpec as P

LS = 5
SR = 4
LCUT = 1600
BLOCK = 16
ALPHA = math.sqrt(math.log(2.0) / math.pi)
EPSILON = 1e-06
HIGHEST = lax.Precision.HIGHEST
HALO = 136
EDGE = 8
LANES = 128
TAPS = [math.exp(-math.pi * (k / (ALPHA * LS)) ** 2) for k in range(-SR, SR + 1)]
VMEM_LIMIT = 24 * 1024 * 1024


def lane_iota(rows):
    return lax.broadcasted_iota(jnp.int32, (rows, LANES), 1)


def pack_kernel(x_ref, top_ref, bot_ref):
    rows, cols = x_ref.shape[1], x_ref.shape[2]
    for j in range(cols // LANES):
        sl = slice(j * LANES, (j + 1) * LANES)
        top_ref[0, j] = x_ref[0, 0:HALO, sl]
        bot_ref[0, j] = x_ref[0, rows - HALO : rows, sl]


def pack(after):
    scans, rows, cols = after.shape
    n_tiles = cols // LANES
    spec = pl.BlockSpec((1, n_tiles, HALO, LANES), lambda s: (s, 0, 0, 0))
    shape = jax.ShapeDtypeStruct((scans, n_tiles, HALO, LANES), jnp.float32)
    return pl.pallas_call(
        pack_kernel,
        grid=(scans,),
        in_specs=[pl.BlockSpec((1, rows, cols), lambda s: (s, 0, 0))],
        out_specs=[spec, spec],
        out_shape=[shape, shape],
        name="pack",
    )(after)


def flip_kernel(x_ref, o_ref):
    rows, cols = x_ref.shape[1], x_ref.shape[2]
    for j in range(cols // LANES):
        for h in range(rows // LANES):
            block = x_ref[0, h * LANES : (h + 1) * LANES, j * LANES : (j + 1) * LANES]
            o_ref[0, h, j * LANES : (j + 1) * LANES, :] = block.T


def flip(x):
    scans, rows, cols = x.shape
    halves = rows // LANES
    return pl.pallas_call(
        flip_kernel,
        grid=(scans,),
        in_specs=[pl.BlockSpec((1, rows, cols), lambda s: (s, 0, 0))],
        out_specs=pl.BlockSpec((1, halves, cols, LANES), lambda s: (s, 0, 0, 0)),
        out_shape=jax.ShapeDtypeStruct((scans, halves, cols, LANES), jnp.float32),
        cost_estimate=pl.CostEstimate(
            flops=x.size, bytes_accessed=8 * x.size, transcendentals=0
        ),
        name="flip",
    )(x)


def scalar_taps(fraction):
    t = fraction.astype(jnp.float32) * (1.0 / 256.0)
    t2 = t * t
    t3 = t2 * t
    return (
        0.5 * (2.0 * t2 - t3 - t),
        0.5 * (3.0 * t3 - 5.0 * t2 + 2.0),
        0.5 * (4.0 * t2 - 3.0 * t3 + t),
        0.5 * (t3 - t2),
    )


def tile_copies(s, groups, after, up, dn, win):
    rows = after.shape[1]
    out = []
    for at, first, n in groups:
        out += [
            (up.at[s, pl.ds(first, n)], win.at[s, pl.ds(at, n), pl.ds(0, HALO), :]),
            (dn.at[s, pl.ds(first, n)], win.at[s, pl.ds(at, n), pl.ds(HALO + rows, HALO), :]),
        ]
        out += [
            (
                after.at[s, :, pl.ds((first + i) * LANES, LANES)],
                win.at[s, at + i, pl.ds(HALO, rows), :],
            )
            for i in range(n)
        ]
    return out


def start_copies(copies, sem):
    for n, (a, b) in enumerate(copies):
        pltpu.make_async_copy(a, b, sem.at[n]).start()


def wait_copies(copies, sem):
    for n, (a, b) in enumerate(copies):
        pltpu.make_async_copy(a, b, sem.at[n]).wait()


def tapped(win, s, tile, first, taps):
    acc = taps[0] * win[s, tile, pl.ds(first, LANES), :]
    for a in range(1, 4):
        acc = acc + taps[a] * win[s, tile, pl.ds(first + a, LANES), :]
    return acc.T


def edge_rows_kernel(prev_ref, next_ref, after, up, dn, left_out, right_out, win, sem):
    scans, halves = left_out.shape[0], left_out.shape[1]
    n_out = after.shape[2] // LANES
    groups = ((0, 0, 2), (2, n_out - 2, 2))
    extra = HALO - LANES

    def copies(s):
        return tile_copies(s, groups, after, up, dn, win)

    for s in range(scans):
        start_copies(copies(s), sem.at[s])

    def one_scan(s, carry):
        wait_copies(copies(s), sem.at[s])

        for ref, base in ((prev_ref, 0), (next_ref, 2)):
            taps = scalar_taps(ref[1, s])
            first = HALO + ref[0, s] - 1
            for h in range(halves):
                a = tapped(win, s, base, first + h * LANES, taps)
                b = tapped(win, s, base + 1, first + h * LANES, taps)
                if base == 0:
                    left_out[s, h, 0:LANES, :] = a
                    left_out[s, h, LANES:HALO, :] = b[0:extra]
                else:
                    right_out[s, h, 0:extra, :] = a[LANES - extra : LANES]
                    right_out[s, h, extra:HALO, :] = b
        return carry

    lax.fori_loop(0, scans, one_scan, 0)


def edge_rows(prev, after_next, after, up, dn):
    scans, rows, cols = after.shape
    halves = rows // LANES
    anywhere = pl.BlockSpec(memory_space=pl.ANY)
    vmem = pl.BlockSpec(memory_space=pltpu.VMEM)
    smem = pl.BlockSpec(memory_space=pltpu.SMEM)
    shape = jax.ShapeDtypeStruct((scans, halves, HALO, LANES), jnp.float32)
    return pl.pallas_call(
        edge_rows_kernel,
        in_specs=[smem, smem] + [anywhere] * 3,
        out_specs=[vmem, vmem],
        out_shape=[shape, shape],
        scratch_shapes=[
            pltpu.VMEM((scans, 4, 2 * HALO + rows, LANES), jnp.float32),
            pltpu.SemaphoreType.DMA((scans, 8)),
        ],
        compiler_params=pltpu.CompilerParams(vmem_limit_bytes=VMEM_LIMIT),
        name="edge_rows",
    )(prev, after_next, after, up, dn)


def own_rows_kernel(mine_ref, after, up, dn, out, win, sem):
    scans, halves, cols = out.shape[0], out.shape[1], out.shape[2]
    n_out = cols // LANES

    def copies(s):
        return tile_copies(s, ((0, 0, n_out),), after, up, dn, win)

    start_copies(copies(0), sem.at[0])

    def one_scan(s, carry):
        wait_copies(copies(s), sem.at[s])

        @pl.when(s + 1 < scans)
        def _():
            start_copies(copies(s + 1), sem.at[s + 1])

        taps = scalar_taps(mine_ref[1, s])
        first = HALO + mine_ref[0, s] - 1

        def two_tiles(i, carry):
            done = [
                tapped(win, s, 2 * i + j, first + h * LANES, taps)
                for j in range(2)
                for h in range(halves)
            ]
            for j in range(2):
                at = pl.multiple_of((2 * i + j) * LANES, LANES)
                for h in range(halves):
                    out[s, h, pl.ds(at, LANES), :] = done[j * halves + h]
            return carry

        lax.fori_loop(0, n_out // 2, two_tiles, 0)
        return carry

    lax.fori_loop(0, scans, one_scan, 0)


def own_rows(mine, after, up, dn):
    scans, rows, cols = after.shape
    halves = rows // LANES
    anywhere = pl.BlockSpec(memory_space=pl.ANY)
    smem = pl.BlockSpec(memory_space=pltpu.SMEM)
    return pl.pallas_call(
        own_rows_kernel,
        in_specs=[smem] + [anywhere] * 3,
        out_specs=pl.BlockSpec(memory_space=pltpu.VMEM),
        out_shape=pltpu.VMEM((scans, halves, cols, LANES), jnp.float32),
        scratch_shapes=[
            pltpu.VMEM((scans, cols // LANES, 2 * HALO + rows, LANES), jnp.float32),
            pltpu.SemaphoreType.DMA((scans, 2 + cols // LANES)),
        ],
        compiler_params=pltpu.CompilerParams(vmem_limit_bytes=VMEM_LIMIT),
        cost_estimate=pl.CostEstimate(
            flops=8 * after.size, bytes_accessed=16 * after.size, transcendentals=0
        ),
        name="own_rows",
    )(mine, after, up, dn)


CB = 64


def resample_kernel(
    offs_ref, fracs_ref, wt_ref, rm_ref, hc_ref,
    own, lcols, rcols, beforet,
    dif, edge_l, edge_r, y_ref,
    win, bef, sums, part, sem,
):
    scans, halves, cols = bef.shape[0], bef.shape[1], bef.shape[2]

    def copies(s):
        return [
            (lcols.at[s], win.at[s, :, pl.ds(0, HALO), :]),
            (own.at[s], win.at[s, :, pl.ds(HALO, cols), :]),
            (rcols.at[s], win.at[s, :, pl.ds(HALO + cols, HALO), :]),
            (beforet.at[s], bef.at[s]),
        ]

    start_copies(copies(0), sem.at[0])
    part[...] = jnp.zeros_like(part)
    sums[...] = jnp.zeros_like(sums)
    n_blocks = cols // BLOCK
    weight = [wt_ref[8 * i : 8 * i + 8, :] for i in range(8)]

    def one_scan(s, carry):
        wait_copies(copies(s), sem.at[s])

        @pl.when(s + 1 < scans)
        def _():
            start_copies(copies(s + 1), sem.at[s + 1])

        ct = scalar_taps(fracs_ref[1, s])
        first = HALO + offs_ref[1, s] - 1

        def col_taps(i, carry):
            q0 = pl.multiple_of(i * CB, CB)
            for h in range(halves):
                acc = ct[0] * win[s, h, pl.ds(first + q0, CB), :]
                for b in range(1, 4):
                    acc = acc + ct[b] * win[s, h, pl.ds(first + q0 + b, CB), :]
                dif[s, h, pl.ds(q0, CB), :] = bef[s, h, pl.ds(q0, CB), :] - acc
            return carry

        lax.fori_loop(0, cols // CB, col_taps, 0)
        for h in range(halves):
            edge_l[s, h] = dif[s, h, 0:EDGE, :]
            edge_r[s, h] = dif[s, h, cols - EDGE : cols, :]

        def block_sums(i, carry):
            for h in range(halves):
                total = []
                for e in range(8):
                    q = pl.multiple_of(i * LANES + e * BLOCK, BLOCK)
                    qa = pl.multiple_of(jnp.maximum(q - 8, 0), 8)
                    qb = pl.multiple_of(jnp.minimum(q + 16, cols - 8), 8)
                    t = weight[0] * dif[s, h, pl.ds(qa, 8), :]
                    t = t + weight[1] * dif[s, h, pl.ds(q, 8), :]
                    t = t + weight[2] * dif[s, h, pl.ds(q + 8, 8), :]
                    t = t + weight[3] * dif[s, h, pl.ds(qb, 8), :]
                    total.append(jnp.sum(t, axis=0, keepdims=True))
                at = pl.multiple_of(i * 8 + 8, 8)
                sums[pl.ds(at, 8), h * LANES : (h + 1) * LANES] = jnp.concatenate(total, axis=0)
            return carry

        lax.fori_loop(0, n_blocks // 8, block_sums, 0)
        for h in range(halves):
            sl = slice(h * LANES, (h + 1) * LANES)
            v = [dif[s, h, 8 * i : 8 * i + 8, :] for i in range(3)]
            w = [dif[s, h, cols - 24 + 8 * i : cols - 16 + 8 * i, :] for i in range(3)]
            rows_at = (
                (7, weight[4] * v[0]),
                (8, weight[5] * v[0] + weight[2] * v[1] + weight[3] * v[2]),
                (7 + n_blocks, weight[0] * w[0] + weight[1] * w[1] + weight[6] * w[2]),
                (8 + n_blocks, weight[7] * w[2]),
            )
            for at, t in rows_at:
                sums[at : at + 1, sl] = jnp.sum(t, axis=0, keepdims=True)
        part[...] += jnp.dot(
            sums[...], rm_ref[s], precision=HIGHEST, preferred_element_type=jnp.float32
        )
        return carry

    lax.fori_loop(0, scans, one_scan, 0)
    y = jnp.dot(hc_ref[...], part[...], precision=HIGHEST, preferred_element_type=jnp.float32)
    ext = hc_ref.shape[0] // y_ref.shape[0]
    for t in range(y_ref.shape[0]):
        y_ref[t] = y[t * ext : (t + 1) * ext, :]


def resample(offs, fracs, wt, rm, hc, ext, own, lcols, rcols, beforet):
    scans, halves, cols, _ = own.shape
    n_col = hc.shape[0] // ext
    anywhere = pl.BlockSpec(memory_space=pl.ANY)
    vmem = pl.BlockSpec(memory_space=pltpu.VMEM)
    smem = pl.BlockSpec(memory_space=pltpu.SMEM)
    return pl.pallas_call(
        resample_kernel,
        in_specs=[smem, smem, vmem, vmem, vmem] + [anywhere] * 4,
        out_specs=[vmem, vmem, vmem, vmem],
        out_shape=[
            pltpu.VMEM((scans, halves, cols, LANES), jnp.float32),
            jax.ShapeDtypeStruct((scans, halves, EDGE, LANES), jnp.float32),
            jax.ShapeDtypeStruct((scans, halves, EDGE, LANES), jnp.float32),
            jax.ShapeDtypeStruct((n_col, ext, LANES), jnp.float32),
        ],
        scratch_shapes=[
            pltpu.VMEM((scans, halves, cols + 2 * HALO, LANES), jnp.float32),
            pltpu.VMEM((scans, halves, cols, LANES), jnp.float32),
            pltpu.VMEM((hc.shape[1], halves * LANES), jnp.float32),
            pltpu.VMEM((hc.shape[1], LANES), jnp.float32),
            pltpu.SemaphoreType.DMA((scans, 4)),
        ],
        compiler_params=pltpu.CompilerParams(vmem_limit_bytes=VMEM_LIMIT),
        name="resample",
    )(offs, fracs, wt, rm, hc, own, lcols, rcols, beforet)


def long_rows_kernel(y_ref, hr_ref, z_ref):
    n_row, scans, ext, _ = z_ref.shape
    p = y_ref[0]
    for t in range(1, y_ref.shape[0]):
        p = p + y_ref[t]
    p = jnp.concatenate([p, jnp.zeros((LANES - p.shape[0], LANES), jnp.float32)], axis=0).T
    for s in range(scans):
        z = jnp.dot(
            hr_ref[...], p[s * ext : (s + 1) * ext, :],
            precision=HIGHEST, preferred_element_type=jnp.float32,
        )
        for t in range(n_row):
            z_ref[t, s] = z[t * ext : (t + 1) * ext, :]


def long_rows(y, hr, scans):
    ext = hr.shape[1]
    vmem = pl.BlockSpec(memory_space=pltpu.VMEM)
    return pl.pallas_call(
        long_rows_kernel,
        in_specs=[vmem, vmem],
        out_specs=vmem,
        out_shape=jax.ShapeDtypeStruct((hr.shape[0] // ext, scans, ext, LANES), jnp.float32),
        name="long_rows",
    )(y, hr)


PAD = 2 * EDGE


def across_kernel(invc_ref, diff, lstrip, rstrip, ac_out, ftop, fbot, buf, acs, sem, osem):
    scans, halves, cols = diff.shape[0], diff.shape[1], diff.shape[2]
    n_out = cols // LANES
    rows = halves * LANES

    def copies(s):
        return [
            (diff.at[s], buf.at[s, :, pl.ds(PAD, cols), :]),
            (lstrip.at[s], buf.at[s, :, pl.ds(PAD - EDGE, EDGE), :]),
            (rstrip.at[s], buf.at[s, :, pl.ds(PAD + cols, EDGE), :]),
        ]

    def fetch(s):
        for n, (a, b) in enumerate(copies(s)):
            pltpu.make_async_copy(a, b, sem.at[s, n]).start()

    fetch(0)
    zero = jnp.zeros((LANES - EDGE, LANES), jnp.float32)

    def filtered(s, h, q, n):
        acc = TAPS[SR] * buf[s, h, pl.ds(q + PAD, n), :]
        for k in range(1, SR + 1):
            acc = acc + TAPS[SR + k] * (
                buf[s, h, pl.ds(q + PAD - k, n), :] + buf[s, h, pl.ds(q + PAD + k, n), :]
            )
        return acc

    def one_scan(s, carry):
        for n, (a, b) in enumerate(copies(s)):
            pltpu.make_async_copy(a, b, sem.at[s, n]).wait()

        @pl.when(s + 1 < scans)
        def _():
            fetch(s + 1)

        for h in range(halves):
            buf[s, h, 0 : PAD - EDGE, :] = zero[0:EDGE]
            buf[s, h, PAD + cols + EDGE :, :] = zero[0:EDGE]
        for h in range(halves):
            sl = slice(h * LANES, (h + 1) * LANES)
            lo = filtered(s, h, -EDGE, EDGE) * invc_ref[0:EDGE, :]
            hi = filtered(s, h, cols, EDGE) * invc_ref[EDGE + cols : 2 * EDGE + cols, :]
            acs[s, 0, sl, :] = jnp.concatenate([zero, lo], axis=0).T
            acs[s, n_out + 1, sl, :] = jnp.concatenate([hi, zero], axis=0).T

        def block(i, carry):
            q0 = pl.multiple_of(i * LANES, LANES)
            inv = invc_ref[pl.ds(q0 + EDGE, LANES), :]
            outs = [(filtered(s, h, q0, LANES) * inv).T for h in range(halves)]
            for h in range(halves):
                acs[s, i + 1, h * LANES : (h + 1) * LANES, :] = outs[h]
            return carry

        lax.fori_loop(0, n_out, block, 0)
        pltpu.make_async_copy(acs.at[s], ac_out.at[s], osem.at[s]).start()
        for j in range(n_out + 2):
            ftop[s, j] = acs[s, j, 0:EDGE, :]
            fbot[s, j] = acs[s, j, rows - EDGE : rows, :]
        return carry

    lax.fori_loop(0, scans, one_scan, 0)
    for s in range(scans):
        pltpu.make_async_copy(acs.at[s], ac_out.at[s], osem.at[s]).wait()


def across(invc, diff, lstrip, rstrip):
    scans, halves, cols, _ = diff.shape
    rows = halves * LANES
    n_wide = cols // LANES + 2
    anywhere = pl.BlockSpec(memory_space=pl.ANY)
    vmem = pl.BlockSpec(memory_space=pltpu.VMEM)
    return pl.pallas_call(
        across_kernel,
        in_specs=[vmem, anywhere, anywhere, anywhere],
        out_specs=[pl.BlockSpec(memory_space=pltpu.HBM), vmem, vmem],
        out_shape=[
            pltpu.HBM((scans, n_wide, rows, LANES), jnp.float32),
            jax.ShapeDtypeStruct((scans, n_wide, EDGE, LANES), jnp.float32),
            jax.ShapeDtypeStruct((scans, n_wide, EDGE, LANES), jnp.float32),
        ],
        scratch_shapes=[
            pltpu.VMEM((scans, halves, cols + 2 * PAD, LANES), jnp.float32),
            pltpu.VMEM((scans, n_wide, rows, LANES), jnp.float32),
            pltpu.SemaphoreType.DMA((scans, 3)),
            pltpu.SemaphoreType.DMA((scans,)),
        ],
        compiler_params=pltpu.CompilerParams(vmem_limit_bytes=VMEM_LIMIT),
        cost_estimate=pl.CostEstimate(
            flops=20 * diff.size, bytes_accessed=8 * diff.size, transcendentals=0
        ),
        name="across",
    )(invc, diff, lstrip, rstrip)


def final_kernel(
    z_ref, uc_ref, invr_ref, mc_ref, mr_ref, across_in, upr, dnr,
    band_ref, slope_ref, sum_ref,
    acs, cu, bd, sem,
):
    s = pl.program_id(0)
    scans, n_wide = acs.shape[0], acs.shape[1]
    rows, cols = band_ref.shape[1], band_ref.shape[2]
    n_out = cols // LANES

    def copies(s):
        return [
            (across_in.at[s], acs.at[s, :, pl.ds(PAD, rows), :]),
            (upr.at[s], acs.at[s, :, pl.ds(PAD - EDGE, EDGE), :]),
            (dnr.at[s], acs.at[s, :, pl.ds(PAD + rows, EDGE), :]),
        ]

    def fetch(s):
        for n, (a, b) in enumerate(copies(s)):
            pltpu.make_async_copy(a, b, sem.at[s, n]).start()

    @pl.when(s == 0)
    def _():
        fetch(0)

        parts = []
        for t in range(scans):
            w = z_ref[0, t]
            for n in range(1, z_ref.shape[0]):
                w = w + z_ref[n, t]
            parts.append(w)
        w = jnp.concatenate(parts, axis=0)
        total = None
        for _ in range(3):
            piece = w.astype(jnp.bfloat16)
            w = w - piece.astype(jnp.float32)
            term = jnp.dot(piece, uc_ref[...], preferred_element_type=jnp.float32)
            total = term if total is None else total + term
        ext = cu.shape[2]
        for t in range(scans):
            for j in range(n_wide):
                cu[t, j] = total[t * ext : (t + 1) * ext, j * LANES : (j + 1) * LANES]

    for n, (a, b) in enumerate(copies(s)):
        pltpu.make_async_copy(a, b, sem.at[s, n]).wait()

    @pl.when(s + 1 < scans)
    def _():
        fetch(s + 1)

    for j in range(n_wide):
        acs[s, j, 0 : PAD - EDGE, :] = jnp.zeros((PAD - EDGE, LANES), jnp.float32)
        acs[s, j, PAD + rows + EDGE :, :] = jnp.zeros((PAD - EDGE, LANES), jnp.float32)

    sub = lax.broadcasted_iota(jnp.int32, (BLOCK, LANES), 0).astype(jnp.float32)
    f = (2.0 * sub + 1.0) * (1.0 / 32.0)

    def band_rows(e, carry):
        base = pl.multiple_of(e * BLOCK, BLOCK)
        inv = invr_ref[pl.ds(base, BLOCK), :]
        for j in range(n_wide):
            acc = TAPS[SR] * acs[s, j, pl.ds(base + EDGE, BLOCK), :]
            for k in range(1, SR + 1):
                acc = acc + TAPS[SR + k] * (
                    acs[s, j, pl.ds(base + EDGE - k, BLOCK), :]
                    + acs[s, j, pl.ds(base + EDGE + k, BLOCK), :]
                )
            a = cu[s, j, pl.ds(e, 1), :]
            b = cu[s, j, pl.ds(e + 1, 1), :]
            bd[j, pl.ds(base, BLOCK), :] = acc * inv - (a + f * (b - a))
        return carry

    lax.fori_loop(0, rows // BLOCK + 1, band_rows, 0)

    lane = lane_iota(BLOCK)
    first = lane >= 1
    last = lane < LANES - 1

    def slope_rows(c, carry):
        s1, s2 = carry
        base = pl.multiple_of(c * BLOCK, BLOCK)
        here = [bd[j, pl.ds(base + EDGE, BLOCK), :] for j in range(n_wide)]
        fwd = [pltpu.roll(t, LANES - 1, 1) for t in here[1:]]
        bwd = [pltpu.roll(t, 1, 1) for t in here[:-1]]
        mr = mr_ref[pl.ds(base, BLOCK), :]
        for j in range(n_out):
            so = slice(j * LANES, (j + 1) * LANES)
            gc = jnp.where(last, fwd[j], fwd[j + 1]) - jnp.where(first, bwd[j + 1], bwd[j])
            gc = gc * mc_ref[0:1, so]
            gr = (
                bd[j + 1, pl.ds(base + EDGE + 1, BLOCK), :]
                - bd[j + 1, pl.ds(base + EDGE - 1, BLOCK), :]
            ) * mr
            sq = gc * gc + gr * gr
            v = here[j + 1]
            band_ref[0, pl.ds(base, BLOCK), so] = v
            slope_ref[0, pl.ds(base, BLOCK), so] = sq
            s1 = s1 + v * v
            s2 = s2 + sq
        return s1, s2

    zero = jnp.zeros((BLOCK, LANES), jnp.float32)
    s1, s2 = lax.fori_loop(0, rows // BLOCK, slope_rows, (zero, zero))
    sum_ref[0, 0:1, :] = jnp.sum(s1, axis=0, keepdims=True)
    sum_ref[0, 1:2, :] = jnp.sum(s2, axis=0, keepdims=True)


def final(z, uc, invr, mc, mr, ac, upr, dnr):
    scans, n_wide, rows, _ = ac.shape
    cols = mc.shape[1]
    n_row, _, ext, _ = z.shape
    const2 = lambda s: (0, 0)
    one = lambda s: (s, 0, 0)
    anywhere = pl.BlockSpec(memory_space=pl.ANY)
    return pl.pallas_call(
        final_kernel,
        grid=(scans,),
        in_specs=[
            pl.BlockSpec(z.shape, lambda s: (0, 0, 0, 0)),
            pl.BlockSpec(uc.shape, const2),
            pl.BlockSpec(invr.shape, const2),
            pl.BlockSpec(mc.shape, const2),
            pl.BlockSpec(mr.shape, const2),
            pl.BlockSpec(memory_space=pltpu.HBM),
            anywhere,
            anywhere,
        ],
        out_specs=[
            pl.BlockSpec((1, rows, cols), one),
            pl.BlockSpec((1, rows, cols), one),
            pl.BlockSpec((1, 2, LANES), one),
        ],
        out_shape=[
            jax.ShapeDtypeStruct((scans, rows, cols), jnp.float32),
            jax.ShapeDtypeStruct((scans, rows, cols), jnp.float32),
            jax.ShapeDtypeStruct((scans, 2, LANES), jnp.float32),
        ],
        scratch_shapes=[
            pltpu.VMEM((scans, n_wide, rows + 2 * PAD, LANES), jnp.float32),
            pltpu.VMEM((scans, n_wide, ext, LANES), jnp.float32),
            pltpu.VMEM((n_wide, rows + 2 * EDGE, LANES), jnp.float32),
            pltpu.SemaphoreType.DMA((scans, 3)),
        ],
        compiler_params=pltpu.CompilerParams(vmem_limit_bytes=VMEM_LIMIT),
        name="final",
    )(z, uc, invr, mc, mr, ac, upr, dnr)


def window_weight(index, count):
    total = jnp.zeros(index.shape, jnp.float32)
    for k in range(-SR, SR + 1):
        inside = (index + k >= 0) & (index + k < count)
        total = total + jnp.where(inside, TAPS[k + SR], 0.0)
    return total


def mean_matrix(start, length, count, width):
    fine = start + lax.broadcasted_iota(jnp.int32, (length, 1), 0)
    blocks = start // BLOCK - 1 + lax.broadcasted_iota(jnp.int32, (1, width), 1)
    valid = lax.broadcasted_iota(jnp.int32, (1, width), 1) < length // BLOCK + 2
    total = jnp.zeros((length, width), jnp.float32)
    for k in range(-SR, SR + 1):
        other = fine + k
        inside = (other >= 0) & (other < count)
        coef = jnp.where(inside, TAPS[k + SR] / (BLOCK * window_weight(other, count)), 0.0)
        total = total + jnp.where((other // BLOCK == blocks) & valid, coef, 0.0)
    return total


def mean_weights(start, length, count):
    b = BLOCK
    cases = (
        (8 * b - 8, 8), (8 * b, 8), (8 * b + 8, 8), (9 * b, 8),
        (0, -1), (0, 0), (length - 8, length // b - 1), (length - 8, length // b),
    )
    base = jnp.array([c[0] for c in cases], jnp.int32)[:, None]
    block = jnp.array([c[1] for c in cases], jnp.int32)[:, None] + start // b
    fine = start + base + jnp.arange(8, dtype=jnp.int32)[None, :]
    total = jnp.zeros(fine.shape, jnp.float32)
    for k in range(-SR, SR + 1):
        other = fine + k
        inside = (other >= 0) & (other < count) & (other // b == block)
        total = total + jnp.where(inside, TAPS[k + SR] / (b * window_weight(other, count)), 0.0)
    return jnp.broadcast_to(total.reshape(64, 1), (64, LANES))


def gauss(distance):
    scaled = (distance * BLOCK).astype(jnp.float32) / (ALPHA * LCUT)
    return jnp.exp(-math.pi * scaled * scaled)


def long_matrix(start_block, per_tile, tiles, src_ext, src_first, ext):
    count = per_tile * tiles
    i = jnp.arange(src_ext, dtype=jnp.int32)
    src = start_block - src_first + i
    src_ok = (i >= src_first - 1) & (i <= src_first + per_tile)
    e = jnp.arange(ext, dtype=jnp.int32)
    tgt = (jnp.arange(tiles, dtype=jnp.int32)[:, None] * per_tile - 1 + e[None, :]).reshape(-1)
    tgt = jnp.clip(tgt, 0, count - 1)
    norm = jnp.sum(gauss(jnp.arange(count, dtype=jnp.int32)[None, :] - tgt[:, None]), axis=1)
    m = gauss(src[None, :] - tgt[:, None]) / norm[:, None]
    return jnp.where(src_ok[None, :], m, 0.0)


def upsample_cols(per_tile, wide):
    q = lax.broadcasted_iota(jnp.int32, (LANES, wide), 1) - LANES
    num = 2 * q + 1 - BLOCK
    low = num // (2 * BLOCK)
    frac = (num - low * (2 * BLOCK)).astype(jnp.float32) / (2.0 * BLOCK)
    e = lax.broadcasted_iota(jnp.int32, (LANES, wide), 0)
    near = (q >= -1) & (q <= per_tile * BLOCK)
    m = jnp.where(e == low + 1, 1.0 - frac, 0.0) + jnp.where(e == low + 2, frac, 0.0)
    return jnp.where(near, m, 0.0).astype(jnp.bfloat16)


def in_hbm(x):
    return pltpu.with_memory_space_constraint(x, pltpu.HBM)


def body(before_scan, after_scan, drift_offsets, drift_fractions):
    scans, rows, cols = before_scan.shape
    n_row, n_col = lax.axis_size("row"), lax.axis_size("col")
    row, col = lax.axis_index("row"), lax.axis_index("col")
    offs = drift_offsets.reshape(2, scans)
    fracs = drift_fractions.reshape(2, scans)
    row_down = [(i, i + 1) for i in range(n_row - 1)]
    row_up = [(j, i) for i, j in row_down]
    col_down = [(i, i + 1) for i in range(n_col - 1)]
    col_up = [(j, i) for i, j in col_down]

    top, bot = pack(after_scan)
    up = lax.ppermute(bot, "row", row_down)
    dn = lax.ppermute(top, "row", row_up)
    wide = cols + 2 * LANES
    ext_r, ext_c = 24, 72
    wt = mean_weights(col * cols, cols, n_col * cols)
    rm = mean_matrix(row * rows, rows, n_row * rows, ext_r)
    rm = jnp.stack([jnp.pad(rm, ((0, 0), (s * ext_r, LANES - (s + 1) * ext_r))) for s in range(scans)])
    hc = long_matrix(col * (cols // BLOCK), cols // BLOCK, n_col, cols // BLOCK + 16, 8, ext_c)
    hr = long_matrix(row * (rows // BLOCK), rows // BLOCK, n_row, ext_r, 1, ext_r)
    uc = upsample_cols(cols // BLOCK, wide)
    qg = col * cols - EDGE + jnp.arange(cols + 2 * EDGE, dtype=jnp.int32)
    near = (qg >= col * cols - 1) & (qg <= (col + 1) * cols)
    inv = jnp.where(near, 1.0 / jnp.where(near, window_weight(qg, n_col * cols), 1.0), 0.0)
    inv = jnp.broadcast_to(inv[:, None], (cols + 2 * EDGE, LANES))
    pg = row * rows - EDGE + jnp.arange(rows + 2 * EDGE, dtype=jnp.int32)
    nearr = (pg >= row * rows - 1) & (pg <= (row + 1) * rows)
    invr = jnp.where(nearr, 1.0 / jnp.where(nearr, window_weight(pg, n_row * rows), 1.0), 0.0)
    invr = jnp.broadcast_to(invr[:, None], (rows + 2 * EDGE, LANES))
    qi = col * cols + jnp.arange(cols, dtype=jnp.int32)
    mc = ((qi >= 1) & (qi <= n_col * cols - 2)).astype(jnp.float32)[None, :]
    pi = row * rows + jnp.arange(rows, dtype=jnp.int32)
    mr = ((pi >= 1) & (pi <= n_row * rows - 2)).astype(jnp.float32)
    mr = jnp.broadcast_to(mr[:, None], (rows, LANES))

    mine = jnp.stack([offs[0], fracs[0]])
    mine, wt, rm, hc, hr, uc, inv, invr, mc, mr = lax.optimization_barrier(
        (mine, wt, rm, hc, hr, uc, inv, invr, mc, mr)
    )
    prev = lax.ppermute(mine, "col", col_down)
    following = lax.ppermute(mine, "col", col_up)
    left, right = edge_rows(prev, following, after_scan, up, dn)
    lcols = lax.ppermute(right, "col", col_down)
    rcols = lax.ppermute(left, "col", col_up)
    own = own_rows(mine, after_scan, up, dn)
    beforet = in_hbm(flip(lax.optimization_barrier((before_scan, left))[0]))
    diff, edge_l, edge_r, y = resample(
        offs, fracs, wt, rm, hc, ext_c, own, lcols, rcols, beforet
    )
    lstrip = lax.ppermute(edge_r, "col", col_down)
    rstrip = lax.ppermute(edge_l, "col", col_up)
    ac, ftop, fbot = across(inv, diff, lstrip, rstrip)
    y, ftop, fbot = lax.optimization_barrier((y, ftop, fbot))
    y = lax.all_to_all(y, "col", 0, 0, tiled=True)
    upr = lax.ppermute(fbot, "row", row_down)
    dnr = lax.ppermute(ftop, "row", row_up)
    z = long_rows(y, hr, scans)
    z = lax.all_to_all(z, "row", 0, 0, tiled=True)
    band, slope, sums = final(z, uc, invr, mc, mr, in_hbm(ac), upr, dnr)

    mine = jnp.sum(sums, axis=2).T.reshape(1, 2 * scans)
    mine = jnp.broadcast_to(mine[:, None, :], (n_row * n_col, 1, 2 * scans))
    every = lax.all_to_all(mine, ("row", "col"), 0, 0, tiled=True)
    total = jnp.sum(every, axis=(0, 1)).reshape(2, scans)
    cells = n_row * rows * n_col * cols
    return band, slope, jnp.sqrt(total / cells + EPSILON)


def solution(mesh):
    in_specs = (
        P(None, "row", "col"),
        P(None, "row", "col"),
        P(None, None, "row", "col"),
        P(None, None, "row", "col"),
    )
    out_specs = (P(None, "row", "col"), P(None, "row", "col"), P())
    return jax.shard_map(body, mesh=mesh, in_specs=in_specs, out_specs=out_specs, check_vma=False)
```

```python
import functools
import math

import jax
import jax.numpy as jnp
from jax import lax
from jax.experimental import pallas as pl
from jax.experimental.pallas import tpu as pltpu
from jax.sharding import PartitionSpec as P

LS = 5
SR = 4
LCUT = 1600
BLOCK = 16
ALPHA = math.sqrt(math.log(2.0) / math.pi)
EPSILON = 1e-06
HIGHEST = lax.Precision.HIGHEST
HALO = 136
EDGE = 8
LANES = 128
TAPS = [math.exp(-math.pi * (k / (ALPHA * LS)) ** 2) for k in range(-SR, SR + 1)]
VMEM_LIMIT = 24 * 1024 * 1024


def pack_kernel(x_ref, top, bot, buf, sem):
    scans, rows, cols = buf.shape

    def fetch(s):
        return pltpu.make_async_copy(x_ref.at[s], buf.at[s], sem.at[s])

    for s in range(scans):
        fetch(s).start()

    def one_scan(s, carry):
        fetch(s).wait()
        for j in range(cols // LANES):
            sl = slice(j * LANES, (j + 1) * LANES)
            top[s, j] = buf[s, 0:HALO, sl]
            bot[s, j] = buf[s, rows - HALO : rows, sl]
        return carry

    lax.fori_loop(0, scans, one_scan, 0)


def pack(after):
    scans, rows, cols = after.shape
    vmem = pl.BlockSpec(memory_space=pltpu.VMEM)
    strip = pltpu.VMEM((scans, cols // LANES, HALO, LANES), jnp.float32)
    return pl.pallas_call(
        pack_kernel,
        in_specs=[pl.BlockSpec(memory_space=pltpu.HBM)],
        out_specs=[vmem, vmem],
        out_shape=[strip, strip],
        scratch_shapes=[
            pltpu.VMEM((scans, rows, cols), jnp.float32),
            pltpu.SemaphoreType.DMA((scans,)),
        ],
        compiler_params=pltpu.CompilerParams(vmem_limit_bytes=VMEM_LIMIT),
        name="pack",
    )(after)


def flip_kernel(x_ref, o_ref):
    rows, cols = x_ref.shape[1], x_ref.shape[2]
    for j in range(cols // LANES):
        for h in range(rows // LANES):
            block = x_ref[0, h * LANES : (h + 1) * LANES, j * LANES : (j + 1) * LANES]
            o_ref[0, h, j * LANES : (j + 1) * LANES, :] = block.T


def flip(x):
    scans, rows, cols = x.shape
    halves = rows // LANES
    return pl.pallas_call(
        flip_kernel,
        grid=(scans,),
        in_specs=[pl.BlockSpec((1, rows, cols), lambda s: (s, 0, 0))],
        out_specs=pl.BlockSpec((1, halves, cols, LANES), lambda s: (s, 0, 0, 0)),
        out_shape=jax.ShapeDtypeStruct((scans, halves, cols, LANES), jnp.float32),
        cost_estimate=pl.CostEstimate(
            flops=x.size, bytes_accessed=8 * x.size, transcendentals=0
        ),
        name="flip",
    )(x)


def scalar_taps(fraction):
    t = fraction.astype(jnp.float32) * (1.0 / 256.0)
    t2 = t * t
    t3 = t2 * t
    return (
        0.5 * (2.0 * t2 - t3 - t),
        0.5 * (3.0 * t3 - 5.0 * t2 + 2.0),
        0.5 * (4.0 * t2 - 3.0 * t3 + t),
        0.5 * (t3 - t2),
    )


def tile_copies(s, groups, after, up, dn, win):
    rows = after.shape[1]
    out = []
    for at, first, n in groups:
        out += [
            (up.at[s, pl.ds(first, n)], win.at[s, pl.ds(at, n), pl.ds(0, HALO), :]),
            (dn.at[s, pl.ds(first, n)], win.at[s, pl.ds(at, n), pl.ds(HALO + rows, HALO), :]),
        ]
        out += [
            (
                after.at[s, :, pl.ds((first + i) * LANES, LANES)],
                win.at[s, at + i, pl.ds(HALO, rows), :],
            )
            for i in range(n)
        ]
    return out


def start_copies(copies, sem):
    for n, (a, b) in enumerate(copies):
        pltpu.make_async_copy(a, b, sem.at[n]).start()


def wait_copies(copies, sem):
    for n, (a, b) in enumerate(copies):
        pltpu.make_async_copy(a, b, sem.at[n]).wait()


def tapped(win, s, tile, first, taps):
    acc = taps[0] * win[s, tile, pl.ds(first, LANES), :]
    for a in range(1, 4):
        acc = acc + taps[a] * win[s, tile, pl.ds(first + a, LANES), :]
    return acc.T


def edge_rows_kernel(prev_ref, next_ref, after, up, dn, left_out, right_out, win, sem):
    scans, halves = left_out.shape[0], left_out.shape[1]
    n_out = after.shape[2] // LANES
    groups = ((0, 0, 2), (2, n_out - 2, 2))
    extra = HALO - LANES

    def copies(s):
        return tile_copies(s, groups, after, up, dn, win)

    for s in range(scans):
        start_copies(copies(s), sem.at[s])

    def one_scan(s, carry):
        wait_copies(copies(s), sem.at[s])

        for ref, base in ((prev_ref, 0), (next_ref, 2)):
            taps = scalar_taps(ref[1, s])
            first = HALO + ref[0, s] - 1
            for h in range(halves):
                a = tapped(win, s, base, first + h * LANES, taps)
                b = tapped(win, s, base + 1, first + h * LANES, taps)
                if base == 0:
                    left_out[s, h, 0:LANES, :] = a
                    left_out[s, h, LANES:HALO, :] = b[0:extra]
                else:
                    right_out[s, h, 0:extra, :] = a[LANES - extra : LANES]
                    right_out[s, h, extra:HALO, :] = b
        return carry

    lax.fori_loop(0, scans, one_scan, 0)


def edge_rows(prev, after_next, after, up, dn):
    scans, rows, cols = after.shape
    halves = rows // LANES
    anywhere = pl.BlockSpec(memory_space=pl.ANY)
    vmem = pl.BlockSpec(memory_space=pltpu.VMEM)
    smem = pl.BlockSpec(memory_space=pltpu.SMEM)
    shape = jax.ShapeDtypeStruct((scans, halves, HALO, LANES), jnp.float32)
    return pl.pallas_call(
        edge_rows_kernel,
        in_specs=[smem, smem] + [anywhere] * 3,
        out_specs=[vmem, vmem],
        out_shape=[shape, shape],
        scratch_shapes=[
            pltpu.VMEM((scans, 4, 2 * HALO + rows, LANES), jnp.float32),
            pltpu.SemaphoreType.DMA((scans, 8)),
        ],
        compiler_params=pltpu.CompilerParams(vmem_limit_bytes=VMEM_LIMIT),
        name="edge_rows",
    )(prev, after_next, after, up, dn)


def own_rows_kernel(mine_ref, after, up, dn, out, win, sem):
    scans, halves, cols = out.shape[0], out.shape[1], out.shape[2]
    n_out = cols // LANES

    def copies(s):
        return tile_copies(s, ((0, 0, n_out),), after, up, dn, win)

    start_copies(copies(0), sem.at[0])

    def one_scan(s, carry):
        wait_copies(copies(s), sem.at[s])

        @pl.when(s + 1 < scans)
        def _():
            start_copies(copies(s + 1), sem.at[s + 1])

        taps = scalar_taps(mine_ref[1, s])
        first = HALO + mine_ref[0, s] - 1

        def two_tiles(i, carry):
            done = [
                tapped(win, s, 2 * i + j, first + h * LANES, taps)
                for j in range(2)
                for h in range(halves)
            ]
            for j in range(2):
                at = pl.multiple_of((2 * i + j) * LANES, LANES)
                for h in range(halves):
                    out[s, h, pl.ds(at, LANES), :] = done[j * halves + h]
            return carry

        lax.fori_loop(0, n_out // 2, two_tiles, 0)
        return carry

    lax.fori_loop(0, scans, one_scan, 0)


def own_rows(mine, after, up, dn):
    scans, rows, cols = after.shape
    halves = rows // LANES
    anywhere = pl.BlockSpec(memory_space=pl.ANY)
    smem = pl.BlockSpec(memory_space=pltpu.SMEM)
    return pl.pallas_call(
        own_rows_kernel,
        in_specs=[smem] + [anywhere] * 3,
        out_specs=pl.BlockSpec(memory_space=pltpu.VMEM),
        out_shape=pltpu.VMEM((scans, halves, cols, LANES), jnp.float32),
        scratch_shapes=[
            pltpu.VMEM((scans, cols // LANES, 2 * HALO + rows, LANES), jnp.float32),
            pltpu.SemaphoreType.DMA((scans, 2 + cols // LANES)),
        ],
        compiler_params=pltpu.CompilerParams(vmem_limit_bytes=VMEM_LIMIT),
        cost_estimate=pl.CostEstimate(
            flops=8 * after.size, bytes_accessed=16 * after.size, transcendentals=0
        ),
        name="own_rows",
    )(mine, after, up, dn)


CB = 64


def resample_kernel(
    offs_ref, fracs_ref, wt_ref, rm_ref, hc_ref,
    own, lcols, rcols, beforet,
    diff_out, y_ref,
    win, bef, dif, sums, part, sem, osem,
):
    scans, halves, cols = bef.shape[0], bef.shape[1], bef.shape[2]

    def copies(s):
        return [
            (lcols.at[s], win.at[s, :, pl.ds(0, HALO), :]),
            (own.at[s], win.at[s, :, pl.ds(HALO, cols), :]),
            (rcols.at[s], win.at[s, :, pl.ds(HALO + cols, HALO), :]),
            (beforet.at[s], bef.at[s]),
        ]

    start_copies(copies(0), sem.at[0])
    part[...] = jnp.zeros_like(part)
    col = lax.axis_index("col")
    n_col = y_ref.shape[0]
    ext = hc_ref.shape[0] // n_col
    y_ref[:, ext:, :] = jnp.zeros((n_col, y_ref.shape[1] - ext, LANES), jnp.float32)
    sums[...] = jnp.zeros_like(sums)
    n_blocks = cols // BLOCK
    weight = [wt_ref[8 * i : 8 * i + 8, :] for i in range(8)]

    def one_scan(s, carry):
        wait_copies(copies(s), sem.at[s])

        @pl.when(s + 1 < scans)
        def _():
            start_copies(copies(s + 1), sem.at[s + 1])

        ct = scalar_taps(fracs_ref[1, s])
        first = HALO + offs_ref[1, s] - 1

        def col_taps(i, carry):
            q0 = pl.multiple_of(i * CB, CB)
            for h in range(halves):
                acc = ct[0] * win[s, h, pl.ds(first + q0, CB), :]
                for b in range(1, 4):
                    acc = acc + ct[b] * win[s, h, pl.ds(first + q0 + b, CB), :]
                dif[s, h, pl.ds(q0, CB), :] = bef[s, h, pl.ds(q0, CB), :] - acc
            return carry

        lax.fori_loop(0, cols // CB, col_taps, 0)
        pltpu.make_async_copy(dif.at[s], diff_out.at[s], osem.at[s]).start()

        def put_edge(target, first):
            for h in range(halves):
                at = pl.multiple_of(ext + (s * halves + h) * EDGE, EDGE)
                y_ref[target, pl.ds(at, EDGE), :] = dif[s, h, first : first + EDGE, :]

        @pl.when(col > 0)
        def _():
            put_edge(col - 1, 0)

        @pl.when(col < n_col - 1)
        def _():
            put_edge(col + 1, cols - EDGE)


        def block_sums(i, carry):
            for h in range(halves):
                total = []
                for e in range(8):
                    q = pl.multiple_of(i * LANES + e * BLOCK, BLOCK)
                    qa = pl.multiple_of(jnp.maximum(q - 8, 0), 8)
                    qb = pl.multiple_of(jnp.minimum(q + 16, cols - 8), 8)
                    t = weight[0] * dif[s, h, pl.ds(qa, 8), :]
                    t = t + weight[1] * dif[s, h, pl.ds(q, 8), :]
                    t = t + weight[2] * dif[s, h, pl.ds(q + 8, 8), :]
                    t = t + weight[3] * dif[s, h, pl.ds(qb, 8), :]
                    total.append(jnp.sum(t, axis=0, keepdims=True))
                at = pl.multiple_of(i * 8 + 8, 8)
                sums[pl.ds(at, 8), h * LANES : (h + 1) * LANES] = jnp.concatenate(total, axis=0)
            return carry

        lax.fori_loop(0, n_blocks // 8, block_sums, 0)
        for h in range(halves):
            sl = slice(h * LANES, (h + 1) * LANES)
            v = [dif[s, h, 8 * i : 8 * i + 8, :] for i in range(3)]
            w = [dif[s, h, cols - 24 + 8 * i : cols - 16 + 8 * i, :] for i in range(3)]
            rows_at = (
                (7, weight[4] * v[0]),
                (8, weight[5] * v[0] + weight[2] * v[1] + weight[3] * v[2]),
                (7 + n_blocks, weight[0] * w[0] + weight[1] * w[1] + weight[6] * w[2]),
                (8 + n_blocks, weight[7] * w[2]),
            )
            for at, t in rows_at:
                sums[at : at + 1, sl] = jnp.sum(t, axis=0, keepdims=True)
        part[...] += jnp.dot(
            sums[...], rm_ref[s], precision=HIGHEST, preferred_element_type=jnp.float32
        )
        return carry

    lax.fori_loop(0, scans, one_scan, 0)
    y = jnp.dot(hc_ref[...], part[...], precision=HIGHEST, preferred_element_type=jnp.float32)
    for t in range(n_col):
        y_ref[t, 0:ext, :] = y[t * ext : (t + 1) * ext, :]
    for s in range(scans):
        pltpu.make_async_copy(dif.at[s], diff_out.at[s], osem.at[s]).wait()


def resample(offs, fracs, wt, rm, hc, ext, own, lcols, rcols, beforet):
    scans, halves, cols, _ = own.shape
    n_col = hc.shape[0] // ext
    anywhere = pl.BlockSpec(memory_space=pl.ANY)
    vmem = pl.BlockSpec(memory_space=pltpu.VMEM)
    smem = pl.BlockSpec(memory_space=pltpu.SMEM)
    return pl.pallas_call(
        resample_kernel,
        in_specs=[smem, smem, vmem, vmem, vmem] + [anywhere] * 4,
        out_specs=[pl.BlockSpec(memory_space=pltpu.HBM), vmem],
        out_shape=[
            pltpu.HBM((scans, halves, cols, LANES), jnp.float32),
            jax.ShapeDtypeStruct((n_col, ext + scans * halves * EDGE, LANES), jnp.float32),
        ],
        scratch_shapes=[
            pltpu.VMEM((scans, halves, cols + 2 * HALO, LANES), jnp.float32),
            pltpu.VMEM((scans, halves, cols, LANES), jnp.float32),
            pltpu.VMEM((scans, halves, cols, LANES), jnp.float32),
            pltpu.VMEM((hc.shape[1], halves * LANES), jnp.float32),
            pltpu.VMEM((hc.shape[1], LANES), jnp.float32),
            pltpu.SemaphoreType.DMA((scans, 4)),
            pltpu.SemaphoreType.DMA((scans,)),
        ],
        compiler_params=pltpu.CompilerParams(vmem_limit_bytes=VMEM_LIMIT),
        name="resample",
    )(offs, fracs, wt, rm, hc, own, lcols, rcols, beforet)


def long_rows_kernel(ext_c, y_ref, hr_ref, z_ref):
    n_row, scans, ext, _ = z_ref.shape
    p = y_ref[0, 0:ext_c, :]
    for t in range(1, y_ref.shape[0]):
        p = p + y_ref[t, 0:ext_c, :]
    p = jnp.concatenate([p, jnp.zeros((LANES - p.shape[0], LANES), jnp.float32)], axis=0).T
    for s in range(scans):
        z = jnp.dot(
            hr_ref[...], p[s * ext : (s + 1) * ext, :],
            precision=HIGHEST, preferred_element_type=jnp.float32,
        )
        for t in range(n_row):
            z_ref[t, s] = z[t * ext : (t + 1) * ext, :]


def long_rows(y, hr, scans, ext_c):
    ext = hr.shape[1]
    vmem = pl.BlockSpec(memory_space=pltpu.VMEM)
    return pl.pallas_call(
        functools.partial(long_rows_kernel, ext_c),
        in_specs=[vmem, vmem],
        out_specs=vmem,
        out_shape=jax.ShapeDtypeStruct((hr.shape[0] // ext, scans, ext, LANES), jnp.float32),
        name="long_rows",
    )(y, hr)


PAD = 2 * EDGE


def across_kernel(invc_ref, diff, y, ac_out, ftop, fbot, buf, acs, sem, osem):
    scans, halves, cols = diff.shape[0], diff.shape[1], diff.shape[2]
    n_out = cols // LANES
    rows = halves * LANES
    col = lax.axis_index("col")
    before = jnp.maximum(col - 1, 0)
    behind = jnp.minimum(col + 1, y.shape[0] - 1)

    def strip_row(s, h):
        first = y.shape[1] - scans * halves * EDGE
        return pl.multiple_of(first + (s * halves + h) * EDGE, EDGE)

    def copies(s):
        return [
            (diff.at[s], buf.at[s, :, pl.ds(PAD, cols), :]),
        ] + [
            (
                y.at[source, pl.ds(strip_row(s, h), EDGE), :],
                buf.at[s, h, pl.ds(first, EDGE), :],
            )
            for h in range(halves)
            for source, first in ((before, PAD - EDGE), (behind, PAD + cols))
        ]

    def fetch(s):
        for n, (a, b) in enumerate(copies(s)):
            pltpu.make_async_copy(a, b, sem.at[s, n]).start()

    fetch(0)
    zero = jnp.zeros((LANES - EDGE, LANES), jnp.float32)

    def filtered(s, h, q, n):
        acc = TAPS[SR] * buf[s, h, pl.ds(q + PAD, n), :]
        for k in range(1, SR + 1):
            acc = acc + TAPS[SR + k] * (
                buf[s, h, pl.ds(q + PAD - k, n), :] + buf[s, h, pl.ds(q + PAD + k, n), :]
            )
        return acc

    def one_scan(s, carry):
        for n, (a, b) in enumerate(copies(s)):
            pltpu.make_async_copy(a, b, sem.at[s, n]).wait()

        @pl.when(s + 1 < scans)
        def _():
            fetch(s + 1)

        for h in range(halves):
            buf[s, h, 0 : PAD - EDGE, :] = zero[0:EDGE]
            buf[s, h, PAD + cols + EDGE :, :] = zero[0:EDGE]
        for h in range(halves):
            sl = slice(h * LANES, (h + 1) * LANES)
            lo = filtered(s, h, -EDGE, EDGE) * invc_ref[0:EDGE, :]
            hi = filtered(s, h, cols, EDGE) * invc_ref[EDGE + cols : 2 * EDGE + cols, :]
            acs[s, 0, sl, :] = jnp.concatenate([zero, lo], axis=0).T
            acs[s, n_out + 1, sl, :] = jnp.concatenate([hi, zero], axis=0).T

        def block(i, carry):
            q0 = pl.multiple_of(i * LANES, LANES)
            inv = invc_ref[pl.ds(q0 + EDGE, LANES), :]
            outs = [(filtered(s, h, q0, LANES) * inv).T for h in range(halves)]
            for h in range(halves):
                acs[s, i + 1, h * LANES : (h + 1) * LANES, :] = outs[h]
            return carry

        lax.fori_loop(0, n_out, block, 0)
        pltpu.make_async_copy(acs.at[s], ac_out.at[s], osem.at[s]).start()
        for j in range(n_out + 2):
            ftop[s, j] = acs[s, j, 0:EDGE, :]
            fbot[s, j] = acs[s, j, rows - EDGE : rows, :]
        return carry

    lax.fori_loop(0, scans, one_scan, 0)
    for s in range(scans):
        pltpu.make_async_copy(acs.at[s], ac_out.at[s], osem.at[s]).wait()


def across(invc, diff, y):
    scans, halves, cols, _ = diff.shape
    rows = halves * LANES
    n_wide = cols // LANES + 2
    anywhere = pl.BlockSpec(memory_space=pl.ANY)
    vmem = pl.BlockSpec(memory_space=pltpu.VMEM)
    return pl.pallas_call(
        across_kernel,
        in_specs=[vmem, pl.BlockSpec(memory_space=pltpu.HBM), anywhere],
        out_specs=[pl.BlockSpec(memory_space=pltpu.HBM), vmem, vmem],
        out_shape=[
            pltpu.HBM((scans, n_wide, rows, LANES), jnp.float32),
            jax.ShapeDtypeStruct((scans, n_wide, EDGE, LANES), jnp.float32),
            jax.ShapeDtypeStruct((scans, n_wide, EDGE, LANES), jnp.float32),
        ],
        scratch_shapes=[
            pltpu.VMEM((scans, halves, cols + 2 * PAD, LANES), jnp.float32),
            pltpu.VMEM((scans, n_wide, rows, LANES), jnp.float32),
            pltpu.SemaphoreType.DMA((scans, 5)),
            pltpu.SemaphoreType.DMA((scans,)),
        ],
        compiler_params=pltpu.CompilerParams(vmem_limit_bytes=VMEM_LIMIT),
        cost_estimate=pl.CostEstimate(
            flops=20 * diff.size, bytes_accessed=8 * diff.size, transcendentals=0
        ),
        name="across",
    )(invc, diff, y)


def final_kernel(
    z_ref, uc_ref, invr_ref, mc_ref, mr_ref, across_in, upr, dnr,
    band_ref, slope_ref, sum_ref,
    acs, cu, bd, bt, sem,
):
    s = pl.program_id(0)
    scans, n_wide = acs.shape[0], acs.shape[1]
    rows, cols = band_ref.shape[1], band_ref.shape[2]
    n_out = cols // LANES

    def copies(s):
        return [
            (across_in.at[s], acs.at[s, :, pl.ds(PAD, rows), :]),
            (upr.at[s], acs.at[s, :, pl.ds(PAD - EDGE, EDGE), :]),
            (dnr.at[s], acs.at[s, :, pl.ds(PAD + rows, EDGE), :]),
        ]

    def fetch(s):
        for n, (a, b) in enumerate(copies(s)):
            pltpu.make_async_copy(a, b, sem.at[s, n]).start()

    @pl.when(s == 0)
    def _():
        fetch(0)

        parts = []
        for t in range(scans):
            w = z_ref[0, t]
            for n in range(1, z_ref.shape[0]):
                w = w + z_ref[n, t]
            parts.append(w)
        w = jnp.concatenate(parts, axis=0)
        total = None
        for _ in range(3):
            piece = w.astype(jnp.bfloat16)
            w = w - piece.astype(jnp.float32)
            term = jnp.dot(piece, uc_ref[...], preferred_element_type=jnp.float32)
            total = term if total is None else total + term
        ext = cu.shape[2]
        for t in range(scans):
            for j in range(n_wide):
                cu[t, j] = total[t * ext : (t + 1) * ext, j * LANES : (j + 1) * LANES]

    for n, (a, b) in enumerate(copies(s)):
        pltpu.make_async_copy(a, b, sem.at[s, n]).wait()

    @pl.when(s + 1 < scans)
    def _():
        fetch(s + 1)

    for j in range(n_wide):
        acs[s, j, 0 : PAD - EDGE, :] = jnp.zeros((PAD - EDGE, LANES), jnp.float32)
        acs[s, j, PAD + rows + EDGE :, :] = jnp.zeros((PAD - EDGE, LANES), jnp.float32)

    sub = lax.broadcasted_iota(jnp.int32, (BLOCK, LANES), 0).astype(jnp.float32)
    f = (2.0 * sub + 1.0) * (1.0 / 32.0)

    def band_rows(e, carry):
        base = pl.multiple_of(e * BLOCK, BLOCK)
        inv = invr_ref[pl.ds(base, BLOCK), :]
        for j in range(n_wide):
            acc = TAPS[SR] * acs[s, j, pl.ds(base + EDGE, BLOCK), :]
            for k in range(1, SR + 1):
                acc = acc + TAPS[SR + k] * (
                    acs[s, j, pl.ds(base + EDGE - k, BLOCK), :]
                    + acs[s, j, pl.ds(base + EDGE + k, BLOCK), :]
                )
            a = cu[s, j, pl.ds(e, 1), :]
            b = cu[s, j, pl.ds(e + 1, 1), :]
            bd[j, pl.ds(base, BLOCK), :] = acc * inv - (a + f * (b - a))
        return carry

    lax.fori_loop(0, rows // BLOCK + 1, band_rows, 0)

    halves = rows // LANES

    def turn(i, carry):
        done = [
            bd[2 * i + n, EDGE + h * LANES : EDGE + (h + 1) * LANES, :].T
            for n in range(2)
            for h in range(halves)
        ]
        for n in range(2):
            at = pl.multiple_of((2 * i + n) * LANES, LANES)
            for h in range(halves):
                bt[h, pl.ds(at, LANES), :] = done[n * halves + h]
        return carry

    lax.fori_loop(0, n_wide // 2, turn, 0)

    def slope_tile(j, carry):
        s1, s2 = carry
        lanes = pl.ds(pl.multiple_of(j * LANES, LANES), LANES)
        at = pl.multiple_of((j + 1) * LANES, LANES)
        squares = []
        for h in range(halves):
            g = bt[h, pl.ds(at + 1, LANES), :] - bt[h, pl.ds(at - 1, LANES), :]
            squares.append((g * g).T)
        for h in range(halves):
            first = h * LANES
            here = slice(first, first + LANES)
            gr = (
                bd[j + 1, first + EDGE + 1 : first + EDGE + 1 + LANES, :]
                - bd[j + 1, first + EDGE - 1 : first + EDGE - 1 + LANES, :]
            ) * mr_ref[here, :]
            sq = squares[h] * mc_ref[0:1, lanes] + gr * gr
            v = bd[j + 1, first + EDGE : first + EDGE + LANES, :]
            band_ref[0, here, lanes] = v
            slope_ref[0, here, lanes] = sq
            s1 = s1 + jnp.sum((v * v).reshape(BLOCK, 8, LANES), axis=0)
            s2 = s2 + jnp.sum(sq.reshape(BLOCK, 8, LANES), axis=0)
        return s1, s2

    zero = jnp.zeros((8, LANES), jnp.float32)
    s1, s2 = lax.fori_loop(0, n_out, slope_tile, (zero, zero))
    sum_ref[0, 0:1, :] = jnp.sum(s1, axis=0, keepdims=True)
    sum_ref[0, 1:2, :] = jnp.sum(s2, axis=0, keepdims=True)


def final(z, uc, invr, mc, mr, ac, upr, dnr):
    scans, n_wide, rows, _ = ac.shape
    cols = mc.shape[1]
    n_row, _, ext, _ = z.shape
    const2 = lambda s: (0, 0)
    one = lambda s: (s, 0, 0)
    anywhere = pl.BlockSpec(memory_space=pl.ANY)
    return pl.pallas_call(
        final_kernel,
        grid=(scans,),
        in_specs=[
            pl.BlockSpec(z.shape, lambda s: (0, 0, 0, 0)),
            pl.BlockSpec(uc.shape, const2),
            pl.BlockSpec(invr.shape, const2),
            pl.BlockSpec(mc.shape, const2),
            pl.BlockSpec(mr.shape, const2),
            pl.BlockSpec(memory_space=pltpu.HBM),
            anywhere,
            anywhere,
        ],
        out_specs=[
            pl.BlockSpec((1, rows, cols), one),
            pl.BlockSpec((1, rows, cols), one),
            pl.BlockSpec((1, 2, LANES), one),
        ],
        out_shape=[
            jax.ShapeDtypeStruct((scans, rows, cols), jnp.float32),
            jax.ShapeDtypeStruct((scans, rows, cols), jnp.float32),
            jax.ShapeDtypeStruct((scans, 2, LANES), jnp.float32),
        ],
        scratch_shapes=[
            pltpu.VMEM((scans, n_wide, rows + 2 * PAD, LANES), jnp.float32),
            pltpu.VMEM((scans, n_wide, ext, LANES), jnp.float32),
            pltpu.VMEM((n_wide, rows + 2 * EDGE, LANES), jnp.float32),
            pltpu.VMEM((rows // LANES, n_wide * LANES, LANES), jnp.float32),
            pltpu.SemaphoreType.DMA((scans, 3)),
        ],
        compiler_params=pltpu.CompilerParams(vmem_limit_bytes=VMEM_LIMIT),
        name="final",
    )(z, uc, invr, mc, mr, ac, upr, dnr)


def window_weight(index, count):
    total = jnp.zeros(index.shape, jnp.float32)
    for k in range(-SR, SR + 1):
        inside = (index + k >= 0) & (index + k < count)
        total = total + jnp.where(inside, TAPS[k + SR], 0.0)
    return total


def mean_matrix(start, length, count, width):
    fine = start + lax.broadcasted_iota(jnp.int32, (length, 1), 0)
    blocks = start // BLOCK - 1 + lax.broadcasted_iota(jnp.int32, (1, width), 1)
    valid = lax.broadcasted_iota(jnp.int32, (1, width), 1) < length // BLOCK + 2
    total = jnp.zeros((length, width), jnp.float32)
    for k in range(-SR, SR + 1):
        other = fine + k
        inside = (other >= 0) & (other < count)
        coef = jnp.where(inside, TAPS[k + SR] / (BLOCK * window_weight(other, count)), 0.0)
        total = total + jnp.where((other // BLOCK == blocks) & valid, coef, 0.0)
    return total


def mean_weights(start, length, count):
    b = BLOCK
    cases = (
        (8 * b - 8, 8), (8 * b, 8), (8 * b + 8, 8), (9 * b, 8),
        (0, -1), (0, 0), (length - 8, length // b - 1), (length - 8, length // b),
    )
    base = jnp.array([c[0] for c in cases], jnp.int32)[:, None]
    block = jnp.array([c[1] for c in cases], jnp.int32)[:, None] + start // b
    fine = start + base + jnp.arange(8, dtype=jnp.int32)[None, :]
    total = jnp.zeros(fine.shape, jnp.float32)
    for k in range(-SR, SR + 1):
        other = fine + k
        inside = (other >= 0) & (other < count) & (other // b == block)
        total = total + jnp.where(inside, TAPS[k + SR] / (b * window_weight(other, count)), 0.0)
    return jnp.broadcast_to(total.reshape(64, 1), (64, LANES))


def gauss(distance):
    scaled = (distance * BLOCK).astype(jnp.float32) / (ALPHA * LCUT)
    return jnp.exp(-math.pi * scaled * scaled)


def long_matrix(start_block, per_tile, tiles, src_ext, src_first, ext):
    count = per_tile * tiles
    i = jnp.arange(src_ext, dtype=jnp.int32)
    src = start_block - src_first + i
    src_ok = (i >= src_first - 1) & (i <= src_first + per_tile)
    e = jnp.arange(ext, dtype=jnp.int32)
    tgt = (jnp.arange(tiles, dtype=jnp.int32)[:, None] * per_tile - 1 + e[None, :]).reshape(-1)
    tgt = jnp.clip(tgt, 0, count - 1)
    norm = jnp.sum(gauss(jnp.arange(count, dtype=jnp.int32)[None, :] - tgt[:, None]), axis=1)
    m = gauss(src[None, :] - tgt[:, None]) / norm[:, None]
    return jnp.where(src_ok[None, :], m, 0.0)


def upsample_cols(per_tile, wide):
    q = lax.broadcasted_iota(jnp.int32, (LANES, wide), 1) - LANES
    num = 2 * q + 1 - BLOCK
    low = num // (2 * BLOCK)
    frac = (num - low * (2 * BLOCK)).astype(jnp.float32) / (2.0 * BLOCK)
    e = lax.broadcasted_iota(jnp.int32, (LANES, wide), 0)
    near = (q >= -1) & (q <= per_tile * BLOCK)
    m = jnp.where(e == low + 1, 1.0 - frac, 0.0) + jnp.where(e == low + 2, frac, 0.0)
    return jnp.where(near, m, 0.0).astype(jnp.bfloat16)


def in_hbm(x):
    return pltpu.with_memory_space_constraint(x, pltpu.HBM)


def body(before_scan, after_scan, drift_offsets, drift_fractions):
    scans, rows, cols = before_scan.shape
    n_row, n_col = lax.axis_size("row"), lax.axis_size("col")
    row, col = lax.axis_index("row"), lax.axis_index("col")
    offs = drift_offsets.reshape(2, scans)
    fracs = drift_fractions.reshape(2, scans)
    row_down = [(i, i + 1) for i in range(n_row - 1)]
    row_up = [(j, i) for i, j in row_down]
    col_down = [(i, i + 1) for i in range(n_col - 1)]
    col_up = [(j, i) for i, j in col_down]

    top, bot = pack(in_hbm(after_scan))
    up = lax.ppermute(bot, "row", row_down)
    dn = lax.ppermute(top, "row", row_up)
    wide = cols + 2 * LANES
    ext_r, ext_c = 24, 72
    wt = mean_weights(col * cols, cols, n_col * cols)
    rm = mean_matrix(row * rows, rows, n_row * rows, ext_r)
    rm = jnp.stack([jnp.pad(rm, ((0, 0), (s * ext_r, LANES - (s + 1) * ext_r))) for s in range(scans)])
    hc = long_matrix(col * (cols // BLOCK), cols // BLOCK, n_col, cols // BLOCK + 16, 8, ext_c)
    hr = long_matrix(row * (rows // BLOCK), rows // BLOCK, n_row, ext_r, 1, ext_r)
    uc = upsample_cols(cols // BLOCK, wide)
    qg = col * cols - EDGE + jnp.arange(cols + 2 * EDGE, dtype=jnp.int32)
    near = (qg >= col * cols - 1) & (qg <= (col + 1) * cols)
    inv = jnp.where(near, 1.0 / jnp.where(near, window_weight(qg, n_col * cols), 1.0), 0.0)
    inv = jnp.broadcast_to(inv[:, None], (cols + 2 * EDGE, LANES))
    pg = row * rows - EDGE + jnp.arange(rows + 2 * EDGE, dtype=jnp.int32)
    nearr = (pg >= row * rows - 1) & (pg <= (row + 1) * rows)
    invr = jnp.where(nearr, 1.0 / jnp.where(nearr, window_weight(pg, n_row * rows), 1.0), 0.0)
    invr = jnp.broadcast_to(invr[:, None], (rows + 2 * EDGE, LANES))
    qi = col * cols + jnp.arange(cols, dtype=jnp.int32)
    mc = ((qi >= 1) & (qi <= n_col * cols - 2)).astype(jnp.float32)[None, :]
    pi = row * rows + jnp.arange(rows, dtype=jnp.int32)
    mr = ((pi >= 1) & (pi <= n_row * rows - 2)).astype(jnp.float32)
    mr = jnp.broadcast_to(mr[:, None], (rows, LANES))

    mine = jnp.stack([offs[0], fracs[0]])
    mine, wt, rm, hc, hr, uc, inv, invr, mc, mr = lax.optimization_barrier(
        (mine, wt, rm, hc, hr, uc, inv, invr, mc, mr)
    )
    prev = lax.ppermute(mine, "col", col_down)
    following = lax.ppermute(mine, "col", col_up)
    left, right = edge_rows(prev, following, after_scan, up, dn)
    lcols = lax.ppermute(right, "col", col_down)
    rcols = lax.ppermute(left, "col", col_up)
    own = own_rows(mine, after_scan, up, dn)
    beforet = in_hbm(flip(lax.optimization_barrier((before_scan, left))[0]))
    diff, y = resample(offs, fracs, wt, rm, hc, ext_c, own, lcols, rcols, beforet)
    y = lax.all_to_all(y, "col", 0, 0, tiled=True)
    z = long_rows(y, hr, scans, ext_c)
    ac, ftop, fbot = across(inv, in_hbm(diff), y)
    upr = lax.ppermute(fbot, "row", row_down)
    dnr = lax.ppermute(ftop, "row", row_up)
    z = lax.all_to_all(z, "row", 0, 0, tiled=True)
    band, slope, sums = final(z, uc, invr, mc, mr, in_hbm(ac), upr, dnr)

    mine = jnp.sum(sums, axis=2).T.reshape(1, 2 * scans)
    mine = jnp.broadcast_to(mine[:, None, :], (n_row * n_col, 1, 2 * scans))
    every = lax.all_to_all(mine, ("row", "col"), 0, 0, tiled=True)
    total = jnp.sum(every, axis=(0, 1)).reshape(2, scans)
    cells = n_row * rows * n_col * cols
    return band, slope, jnp.sqrt(total / cells + EPSILON)


def solution(mesh):
    in_specs = (
        P(None, "row", "col"),
        P(None, "row", "col"),
        P(None, None, "row", "col"),
        P(None, None, "row", "col"),
    )
    out_specs = (P(None, "row", "col"), P(None, "row", "col"), P())
    return jax.shard_map(body, mesh=mesh, in_specs=in_specs, out_specs=out_specs, check_vma=False)
```

```python
import functools
import math

import jax
import jax.numpy as jnp
from jax import lax
from jax.experimental import pallas as pl
from jax.experimental.pallas import tpu as pltpu
from jax.sharding import PartitionSpec as P

LS = 5
SR = 4
LCUT = 1600
BLOCK = 16
ALPHA = math.sqrt(math.log(2.0) / math.pi)
EPSILON = 1e-06
HIGHEST = lax.Precision.HIGHEST
HALO = 136
EDGE = 8
LANES = 128
TAPS = [math.exp(-math.pi * (k / (ALPHA * LS)) ** 2) for k in range(-SR, SR + 1)]
VMEM_LIMIT = 24 * 1024 * 1024


def pack_kernel(x_ref, top, bot, buf, sem):
    scans, rows, cols = buf.shape

    def fetch(s):
        return pltpu.make_async_copy(x_ref.at[s], buf.at[s], sem.at[s])

    for s in range(scans):
        fetch(s).start()

    def one_scan(s, carry):
        fetch(s).wait()
        for j in range(cols // LANES):
            sl = slice(j * LANES, (j + 1) * LANES)
            top[s, j] = buf[s, 0:HALO, sl]
            bot[s, j] = buf[s, rows - HALO : rows, sl]
        return carry

    lax.fori_loop(0, scans, one_scan, 0)


def pack(after):
    scans, rows, cols = after.shape
    vmem = pl.BlockSpec(memory_space=pltpu.VMEM)
    strip = pltpu.VMEM((scans, cols // LANES, HALO, LANES), jnp.float32)
    return pl.pallas_call(
        pack_kernel,
        in_specs=[pl.BlockSpec(memory_space=pltpu.HBM)],
        out_specs=[vmem, vmem],
        out_shape=[strip, strip],
        scratch_shapes=[
            pltpu.VMEM((scans, rows, cols), jnp.float32),
            pltpu.SemaphoreType.DMA((scans,)),
        ],
        compiler_params=pltpu.CompilerParams(vmem_limit_bytes=VMEM_LIMIT),
        name="pack",
    )(after)


def flip_kernel(x_ref, o_ref):
    rows, cols = x_ref.shape[1], x_ref.shape[2]
    for j in range(cols // LANES):
        for h in range(rows // LANES):
            block = x_ref[0, h * LANES : (h + 1) * LANES, j * LANES : (j + 1) * LANES]
            o_ref[0, h, j * LANES : (j + 1) * LANES, :] = block.T


def flip(x):
    scans, rows, cols = x.shape
    halves = rows // LANES
    return pl.pallas_call(
        flip_kernel,
        grid=(scans,),
        in_specs=[pl.BlockSpec((1, rows, cols), lambda s: (s, 0, 0))],
        out_specs=pl.BlockSpec((1, halves, cols, LANES), lambda s: (s, 0, 0, 0)),
        out_shape=jax.ShapeDtypeStruct((scans, halves, cols, LANES), jnp.float32),
        cost_estimate=pl.CostEstimate(
            flops=x.size, bytes_accessed=8 * x.size, transcendentals=0
        ),
        name="flip",
    )(x)


def scalar_taps(fraction):
    t = fraction.astype(jnp.float32) * (1.0 / 256.0)
    t2 = t * t
    t3 = t2 * t
    return (
        0.5 * (2.0 * t2 - t3 - t),
        0.5 * (3.0 * t3 - 5.0 * t2 + 2.0),
        0.5 * (4.0 * t2 - 3.0 * t3 + t),
        0.5 * (t3 - t2),
    )


def tile_copies(s, groups, after, up, dn, win):
    rows = after.shape[1]
    out = []
    for at, first, n in groups:
        out += [
            (up.at[s, pl.ds(first, n)], win.at[s, pl.ds(at, n), pl.ds(0, HALO), :]),
            (dn.at[s, pl.ds(first, n)], win.at[s, pl.ds(at, n), pl.ds(HALO + rows, HALO), :]),
        ]
        out += [
            (
                after.at[s, :, pl.ds((first + i) * LANES, LANES)],
                win.at[s, at + i, pl.ds(HALO, rows), :],
            )
            for i in range(n)
        ]
    return out


def start_copies(copies, sem):
    for n, (a, b) in enumerate(copies):
        pltpu.make_async_copy(a, b, sem.at[n]).start()


def wait_copies(copies, sem):
    for n, (a, b) in enumerate(copies):
        pltpu.make_async_copy(a, b, sem.at[n]).wait()


def tapped(win, s, tile, first, taps):
    acc = taps[0] * win[s, tile, pl.ds(first, LANES), :]
    for a in range(1, 4):
        acc = acc + taps[a] * win[s, tile, pl.ds(first + a, LANES), :]
    return acc.T


def edge_rows_kernel(prev_ref, next_ref, after, up, dn, left_out, right_out, win, sem):
    scans, halves = left_out.shape[0], left_out.shape[1]
    n_out = after.shape[2] // LANES
    groups = ((0, 0, 2), (2, n_out - 2, 2))
    extra = HALO - LANES

    def copies(s):
        return tile_copies(s, groups, after, up, dn, win)

    for s in range(scans):
        start_copies(copies(s), sem.at[s])

    def one_scan(s, carry):
        wait_copies(copies(s), sem.at[s])

        for ref, base in ((prev_ref, 0), (next_ref, 2)):
            taps = scalar_taps(ref[1, s])
            first = HALO + ref[0, s] - 1
            for h in range(halves):
                a = tapped(win, s, base, first + h * LANES, taps)
                b = tapped(win, s, base + 1, first + h * LANES, taps)
                if base == 0:
                    left_out[s, h, 0:LANES, :] = a
                    left_out[s, h, LANES:HALO, :] = b[0:extra]
                else:
                    right_out[s, h, 0:extra, :] = a[LANES - extra : LANES]
                    right_out[s, h, extra:HALO, :] = b
        return carry

    lax.fori_loop(0, scans, one_scan, 0)


def edge_rows(prev, after_next, after, up, dn):
    scans, rows, cols = after.shape
    halves = rows // LANES
    anywhere = pl.BlockSpec(memory_space=pl.ANY)
    vmem = pl.BlockSpec(memory_space=pltpu.VMEM)
    smem = pl.BlockSpec(memory_space=pltpu.SMEM)
    shape = jax.ShapeDtypeStruct((scans, halves, HALO, LANES), jnp.float32)
    return pl.pallas_call(
        edge_rows_kernel,
        in_specs=[smem, smem] + [anywhere] * 3,
        out_specs=[vmem, vmem],
        out_shape=[shape, shape],
        scratch_shapes=[
            pltpu.VMEM((scans, 4, 2 * HALO + rows, LANES), jnp.float32),
            pltpu.SemaphoreType.DMA((scans, 8)),
        ],
        compiler_params=pltpu.CompilerParams(vmem_limit_bytes=VMEM_LIMIT),
        name="edge_rows",
    )(prev, after_next, after, up, dn)


def own_rows_kernel(mine_ref, after, up, dn, out, win, sem):
    scans, halves, cols = out.shape[0], out.shape[1], out.shape[2]
    n_out = cols // LANES

    def copies(s):
        return tile_copies(s, ((0, 0, n_out),), after, up, dn, win)

    start_copies(copies(0), sem.at[0])

    def one_scan(s, carry):
        wait_copies(copies(s), sem.at[s])

        @pl.when(s + 1 < scans)
        def _():
            start_copies(copies(s + 1), sem.at[s + 1])

        taps = scalar_taps(mine_ref[1, s])
        first = HALO + mine_ref[0, s] - 1

        def two_tiles(i, carry):
            done = [
                tapped(win, s, 2 * i + j, first + h * LANES, taps)
                for j in range(2)
                for h in range(halves)
            ]
            for j in range(2):
                at = pl.multiple_of((2 * i + j) * LANES, LANES)
                for h in range(halves):
                    out[s, h, pl.ds(at, LANES), :] = done[j * halves + h]
            return carry

        lax.fori_loop(0, n_out // 2, two_tiles, 0)
        return carry

    lax.fori_loop(0, scans, one_scan, 0)


def own_rows(mine, after, up, dn):
    scans, rows, cols = after.shape
    halves = rows // LANES
    anywhere = pl.BlockSpec(memory_space=pl.ANY)
    smem = pl.BlockSpec(memory_space=pltpu.SMEM)
    return pl.pallas_call(
        own_rows_kernel,
        in_specs=[smem] + [anywhere] * 3,
        out_specs=pl.BlockSpec(memory_space=pltpu.VMEM),
        out_shape=pltpu.VMEM((scans, halves, cols, LANES), jnp.float32),
        scratch_shapes=[
            pltpu.VMEM((scans, cols // LANES, 2 * HALO + rows, LANES), jnp.float32),
            pltpu.SemaphoreType.DMA((scans, 2 + cols // LANES)),
        ],
        compiler_params=pltpu.CompilerParams(vmem_limit_bytes=VMEM_LIMIT),
        cost_estimate=pl.CostEstimate(
            flops=8 * after.size, bytes_accessed=16 * after.size, transcendentals=0
        ),
        name="own_rows",
    )(mine, after, up, dn)


CB = 64


def resample_kernel(
    offs_ref, fracs_ref, wt_ref, rm_ref, hc_ref,
    own, lcols, rcols, beforet,
    diff_out, y_ref,
    win, bef, dif, sums, part, sem, osem,
):
    scans, halves, cols = bef.shape[0], bef.shape[1], bef.shape[2]

    def copies(s):
        return [
            (lcols.at[s], win.at[s, :, pl.ds(0, HALO), :]),
            (own.at[s], win.at[s, :, pl.ds(HALO, cols), :]),
            (rcols.at[s], win.at[s, :, pl.ds(HALO + cols, HALO), :]),
            (beforet.at[s], bef.at[s]),
        ]

    for s in range(scans):
        start_copies(copies(s), sem.at[s])
    part[...] = jnp.zeros_like(part)
    col = lax.axis_index("col")
    n_col = y_ref.shape[0]
    ext = hc_ref.shape[0] // n_col
    y_ref[:, ext:, :] = jnp.zeros((n_col, y_ref.shape[1] - ext, LANES), jnp.float32)
    sums[...] = jnp.zeros_like(sums)
    n_blocks = cols // BLOCK
    weight = [wt_ref[8 * i : 8 * i + 8, :] for i in range(8)]

    def one_scan(s, carry):
        wait_copies(copies(s), sem.at[s])

        ct = scalar_taps(fracs_ref[1, s])
        first = HALO + offs_ref[1, s] - 1

        def col_taps(i, carry):
            q0 = pl.multiple_of(i * CB, CB)
            for h in range(halves):
                acc = ct[0] * win[s, h, pl.ds(first + q0, CB), :]
                for b in range(1, 4):
                    acc = acc + ct[b] * win[s, h, pl.ds(first + q0 + b, CB), :]
                dif[s, h, pl.ds(q0, CB), :] = bef[s, h, pl.ds(q0, CB), :] - acc
            return carry

        lax.fori_loop(0, cols // CB, col_taps, 0)
        pltpu.make_async_copy(dif.at[s], diff_out.at[s], osem.at[s]).start()

        def put_edge(target, first):
            for h in range(halves):
                at = pl.multiple_of(ext + (s * halves + h) * EDGE, EDGE)
                y_ref[target, pl.ds(at, EDGE), :] = dif[s, h, first : first + EDGE, :]

        @pl.when(col > 0)
        def _():
            put_edge(col - 1, 0)

        @pl.when(col < n_col - 1)
        def _():
            put_edge(col + 1, cols - EDGE)


        def block_sums(i, carry):
            for h in range(halves):
                total = []
                for e in range(8):
                    q = pl.multiple_of(i * LANES + e * BLOCK, BLOCK)
                    qa = pl.multiple_of(jnp.maximum(q - 8, 0), 8)
                    qb = pl.multiple_of(jnp.minimum(q + 16, cols - 8), 8)
                    t = weight[0] * dif[s, h, pl.ds(qa, 8), :]
                    t = t + weight[1] * dif[s, h, pl.ds(q, 8), :]
                    t = t + weight[2] * dif[s, h, pl.ds(q + 8, 8), :]
                    t = t + weight[3] * dif[s, h, pl.ds(qb, 8), :]
                    total.append(jnp.sum(t, axis=0, keepdims=True))
                at = pl.multiple_of(i * 8 + 8, 8)
                sums[pl.ds(at, 8), h * LANES : (h + 1) * LANES] = jnp.concatenate(total, axis=0)
            return carry

        lax.fori_loop(0, n_blocks // 8, block_sums, 0)
        for h in range(halves):
            sl = slice(h * LANES, (h + 1) * LANES)
            v = [dif[s, h, 8 * i : 8 * i + 8, :] for i in range(3)]
            w = [dif[s, h, cols - 24 + 8 * i : cols - 16 + 8 * i, :] for i in range(3)]
            rows_at = (
                (7, weight[4] * v[0]),
                (8, weight[5] * v[0] + weight[2] * v[1] + weight[3] * v[2]),
                (7 + n_blocks, weight[0] * w[0] + weight[1] * w[1] + weight[6] * w[2]),
                (8 + n_blocks, weight[7] * w[2]),
            )
            for at, t in rows_at:
                sums[at : at + 1, sl] = jnp.sum(t, axis=0, keepdims=True)
        part[...] += jnp.dot(
            sums[...], rm_ref[s], precision=HIGHEST, preferred_element_type=jnp.float32
        )
        return carry

    lax.fori_loop(0, scans, one_scan, 0)
    y = jnp.dot(hc_ref[...], part[...], precision=HIGHEST, preferred_element_type=jnp.float32)
    for t in range(n_col):
        y_ref[t, 0:ext, :] = y[t * ext : (t + 1) * ext, :]
    for s in range(scans):
        pltpu.make_async_copy(dif.at[s], diff_out.at[s], osem.at[s]).wait()


def resample(offs, fracs, wt, rm, hc, ext, own, lcols, rcols, beforet):
    scans, halves, cols, _ = own.shape
    n_col = hc.shape[0] // ext
    anywhere = pl.BlockSpec(memory_space=pl.ANY)
    vmem = pl.BlockSpec(memory_space=pltpu.VMEM)
    smem = pl.BlockSpec(memory_space=pltpu.SMEM)
    return pl.pallas_call(
        resample_kernel,
        in_specs=[smem, smem, vmem, vmem, vmem] + [anywhere] * 4,
        out_specs=[pl.BlockSpec(memory_space=pltpu.HBM), vmem],
        out_shape=[
            pltpu.HBM((scans, halves, cols, LANES), jnp.float32),
            jax.ShapeDtypeStruct((n_col, ext + scans * halves * EDGE, LANES), jnp.float32),
        ],
        scratch_shapes=[
            pltpu.VMEM((scans, halves, cols + 2 * HALO, LANES), jnp.float32),
            pltpu.VMEM((scans, halves, cols, LANES), jnp.float32),
            pltpu.VMEM((scans, halves, cols, LANES), jnp.float32),
            pltpu.VMEM((hc.shape[1], halves * LANES), jnp.float32),
            pltpu.VMEM((hc.shape[1], LANES), jnp.float32),
            pltpu.SemaphoreType.DMA((scans, 4)),
            pltpu.SemaphoreType.DMA((scans,)),
        ],
        compiler_params=pltpu.CompilerParams(vmem_limit_bytes=VMEM_LIMIT),
        name="resample",
    )(offs, fracs, wt, rm, hc, own, lcols, rcols, beforet)


def long_rows_kernel(ext_c, y_ref, hr_ref, z_ref):
    n_row, scans, ext, _ = z_ref.shape
    p = y_ref[0, 0:ext_c, :]
    for t in range(1, y_ref.shape[0]):
        p = p + y_ref[t, 0:ext_c, :]
    p = jnp.concatenate([p, jnp.zeros((LANES - p.shape[0], LANES), jnp.float32)], axis=0).T
    for s in range(scans):
        z = jnp.dot(
            hr_ref[...], p[s * ext : (s + 1) * ext, :],
            precision=HIGHEST, preferred_element_type=jnp.float32,
        )
        for t in range(n_row):
            z_ref[t, s] = z[t * ext : (t + 1) * ext, :]


def long_rows(y, hr, scans, ext_c):
    ext = hr.shape[1]
    vmem = pl.BlockSpec(memory_space=pltpu.VMEM)
    return pl.pallas_call(
        functools.partial(long_rows_kernel, ext_c),
        in_specs=[vmem, vmem],
        out_specs=vmem,
        out_shape=jax.ShapeDtypeStruct((hr.shape[0] // ext, scans, ext, LANES), jnp.float32),
        name="long_rows",
    )(y, hr)


PAD = 2 * EDGE


def across_kernel(invc_ref, diff, y, ac_out, ftop, fbot, buf, acs, sem, osem):
    scans, halves, cols = diff.shape[0], diff.shape[1], diff.shape[2]
    n_out = cols // LANES
    rows = halves * LANES
    col = lax.axis_index("col")
    before = jnp.maximum(col - 1, 0)
    behind = jnp.minimum(col + 1, y.shape[0] - 1)

    def strip_row(s, h):
        first = y.shape[1] - scans * halves * EDGE
        return pl.multiple_of(first + (s * halves + h) * EDGE, EDGE)

    def copies(s):
        return [
            (diff.at[s], buf.at[s, :, pl.ds(PAD, cols), :]),
        ] + [
            (
                y.at[source, pl.ds(strip_row(s, h), EDGE), :],
                buf.at[s, h, pl.ds(first, EDGE), :],
            )
            for h in range(halves)
            for source, first in ((before, PAD - EDGE), (behind, PAD + cols))
        ]

    def fetch(s):
        for n, (a, b) in enumerate(copies(s)):
            pltpu.make_async_copy(a, b, sem.at[s, n]).start()

    for s in range(scans):
        fetch(s)
    zero = jnp.zeros((LANES - EDGE, LANES), jnp.float32)

    def filtered(s, h, q, n):
        acc = TAPS[SR] * buf[s, h, pl.ds(q + PAD, n), :]
        for k in range(1, SR + 1):
            acc = acc + TAPS[SR + k] * (
                buf[s, h, pl.ds(q + PAD - k, n), :] + buf[s, h, pl.ds(q + PAD + k, n), :]
            )
        return acc

    def one_scan(s, carry):
        for n, (a, b) in enumerate(copies(s)):
            pltpu.make_async_copy(a, b, sem.at[s, n]).wait()

        for h in range(halves):
            buf[s, h, 0 : PAD - EDGE, :] = zero[0:EDGE]
            buf[s, h, PAD + cols + EDGE :, :] = zero[0:EDGE]
        for h in range(halves):
            sl = slice(h * LANES, (h + 1) * LANES)
            lo = filtered(s, h, -EDGE, EDGE) * invc_ref[0:EDGE, :]
            hi = filtered(s, h, cols, EDGE) * invc_ref[EDGE + cols : 2 * EDGE + cols, :]
            acs[s, 0, sl, :] = jnp.concatenate([zero, lo], axis=0).T
            acs[s, n_out + 1, sl, :] = jnp.concatenate([hi, zero], axis=0).T

        def block(i, carry):
            q0 = pl.multiple_of(i * LANES, LANES)
            inv = invc_ref[pl.ds(q0 + EDGE, LANES), :]
            outs = [(filtered(s, h, q0, LANES) * inv).T for h in range(halves)]
            for h in range(halves):
                acs[s, i + 1, h * LANES : (h + 1) * LANES, :] = outs[h]
            return carry

        lax.fori_loop(0, n_out, block, 0)
        pltpu.make_async_copy(acs.at[s], ac_out.at[s], osem.at[s]).start()
        for j in range(n_out + 2):
            ftop[s, j] = acs[s, j, 0:EDGE, :]
            fbot[s, j] = acs[s, j, rows - EDGE : rows, :]
        return carry

    lax.fori_loop(0, scans, one_scan, 0)
    for s in range(scans):
        pltpu.make_async_copy(acs.at[s], ac_out.at[s], osem.at[s]).wait()


def across(invc, diff, y):
    scans, halves, cols, _ = diff.shape
    rows = halves * LANES
    n_wide = cols // LANES + 2
    anywhere = pl.BlockSpec(memory_space=pl.ANY)
    vmem = pl.BlockSpec(memory_space=pltpu.VMEM)
    return pl.pallas_call(
        across_kernel,
        in_specs=[vmem, pl.BlockSpec(memory_space=pltpu.HBM), anywhere],
        out_specs=[pl.BlockSpec(memory_space=pltpu.HBM), vmem, vmem],
        out_shape=[
            pltpu.HBM((scans, n_wide, rows, LANES), jnp.float32),
            jax.ShapeDtypeStruct((scans, n_wide, EDGE, LANES), jnp.float32),
            jax.ShapeDtypeStruct((scans, n_wide, EDGE, LANES), jnp.float32),
        ],
        scratch_shapes=[
            pltpu.VMEM((scans, halves, cols + 2 * PAD, LANES), jnp.float32),
            pltpu.VMEM((scans, n_wide, rows, LANES), jnp.float32),
            pltpu.SemaphoreType.DMA((scans, 5)),
            pltpu.SemaphoreType.DMA((scans,)),
        ],
        compiler_params=pltpu.CompilerParams(vmem_limit_bytes=VMEM_LIMIT),
        cost_estimate=pl.CostEstimate(
            flops=20 * diff.size, bytes_accessed=8 * diff.size, transcendentals=0
        ),
        name="across",
    )(invc, diff, y)


def final_kernel(
    z_ref, uc_ref, invr_ref, mc_ref, mr_ref, across_in, upr, dnr,
    band_ref, slope_ref, sum_ref,
    acs, cu, bd, bt, sem,
):
    s = pl.program_id(0)
    scans, n_wide = acs.shape[0], acs.shape[1]
    rows, cols = band_ref.shape[1], band_ref.shape[2]
    n_out = cols // LANES

    def copies(s):
        return [
            (across_in.at[s], acs.at[s, :, pl.ds(PAD, rows), :]),
            (upr.at[s], acs.at[s, :, pl.ds(PAD - EDGE, EDGE), :]),
            (dnr.at[s], acs.at[s, :, pl.ds(PAD + rows, EDGE), :]),
        ]

    def fetch(s):
        for n, (a, b) in enumerate(copies(s)):
            pltpu.make_async_copy(a, b, sem.at[s, n]).start()

    @pl.when(s == 0)
    def _():
        for t in range(scans):
            fetch(t)


        parts = []
        for t in range(scans):
            w = z_ref[0, t]
            for n in range(1, z_ref.shape[0]):
                w = w + z_ref[n, t]
            parts.append(w)
        w = jnp.concatenate(parts, axis=0)
        total = None
        for _ in range(3):
            piece = w.astype(jnp.bfloat16)
            w = w - piece.astype(jnp.float32)
            term = jnp.dot(piece, uc_ref[...], preferred_element_type=jnp.float32)
            total = term if total is None else total + term
        ext = cu.shape[2]
        for t in range(scans):
            for j in range(n_wide):
                cu[t, j] = total[t * ext : (t + 1) * ext, j * LANES : (j + 1) * LANES]

    for n, (a, b) in enumerate(copies(s)):
        pltpu.make_async_copy(a, b, sem.at[s, n]).wait()

    for j in range(n_wide):
        acs[s, j, 0 : PAD - EDGE, :] = jnp.zeros((PAD - EDGE, LANES), jnp.float32)
        acs[s, j, PAD + rows + EDGE :, :] = jnp.zeros((PAD - EDGE, LANES), jnp.float32)

    sub = lax.broadcasted_iota(jnp.int32, (BLOCK, LANES), 0).astype(jnp.float32)
    f = (2.0 * sub + 1.0) * (1.0 / 32.0)

    def band_rows(e, carry):
        base = pl.multiple_of(e * BLOCK, BLOCK)
        inv = invr_ref[pl.ds(base, BLOCK), :]
        for j in range(n_wide):
            acc = TAPS[SR] * acs[s, j, pl.ds(base + EDGE, BLOCK), :]
            for k in range(1, SR + 1):
                acc = acc + TAPS[SR + k] * (
                    acs[s, j, pl.ds(base + EDGE - k, BLOCK), :]
                    + acs[s, j, pl.ds(base + EDGE + k, BLOCK), :]
                )
            a = cu[s, j, pl.ds(e, 1), :]
            b = cu[s, j, pl.ds(e + 1, 1), :]
            bd[j, pl.ds(base, BLOCK), :] = acc * inv - (a + f * (b - a))
        return carry

    lax.fori_loop(0, rows // BLOCK + 1, band_rows, 0)

    halves = rows // LANES

    def turn(i, carry):
        done = [
            bd[2 * i + n, EDGE + h * LANES : EDGE + (h + 1) * LANES, :].T
            for n in range(2)
            for h in range(halves)
        ]
        for n in range(2):
            at = pl.multiple_of((2 * i + n) * LANES, LANES)
            for h in range(halves):
                bt[h, pl.ds(at, LANES), :] = done[n * halves + h]
        return carry

    lax.fori_loop(0, n_wide // 2, turn, 0)

    def slope_tile(j, carry):
        s1, s2 = carry
        lanes = pl.ds(pl.multiple_of(j * LANES, LANES), LANES)
        at = pl.multiple_of((j + 1) * LANES, LANES)
        squares = []
        for h in range(halves):
            g = bt[h, pl.ds(at + 1, LANES), :] - bt[h, pl.ds(at - 1, LANES), :]
            squares.append((g * g).T)
        for h in range(halves):
            first = h * LANES
            here = slice(first, first + LANES)
            gr = (
                bd[j + 1, first + EDGE + 1 : first + EDGE + 1 + LANES, :]
                - bd[j + 1, first + EDGE - 1 : first + EDGE - 1 + LANES, :]
            ) * mr_ref[here, :]
            sq = squares[h] * mc_ref[0:1, lanes] + gr * gr
            v = bd[j + 1, first + EDGE : first + EDGE + LANES, :]
            band_ref[0, here, lanes] = v
            slope_ref[0, here, lanes] = sq
            s1 = s1 + jnp.sum((v * v).reshape(BLOCK, 8, LANES), axis=0)
            s2 = s2 + jnp.sum(sq.reshape(BLOCK, 8, LANES), axis=0)
        return s1, s2

    zero = jnp.zeros((8, LANES), jnp.float32)
    s1, s2 = lax.fori_loop(0, n_out, slope_tile, (zero, zero))
    sum_ref[0, 0:1, :] = jnp.sum(s1, axis=0, keepdims=True)
    sum_ref[0, 1:2, :] = jnp.sum(s2, axis=0, keepdims=True)


def final(z, uc, invr, mc, mr, ac, upr, dnr):
    scans, n_wide, rows, _ = ac.shape
    cols = mc.shape[1]
    n_row, _, ext, _ = z.shape
    const2 = lambda s: (0, 0)
    one = lambda s: (s, 0, 0)
    anywhere = pl.BlockSpec(memory_space=pl.ANY)
    return pl.pallas_call(
        final_kernel,
        grid=(scans,),
        in_specs=[
            pl.BlockSpec(z.shape, lambda s: (0, 0, 0, 0)),
            pl.BlockSpec(uc.shape, const2),
            pl.BlockSpec(invr.shape, const2),
            pl.BlockSpec(mc.shape, const2),
            pl.BlockSpec(mr.shape, const2),
            pl.BlockSpec(memory_space=pltpu.HBM),
            anywhere,
            anywhere,
        ],
        out_specs=[
            pl.BlockSpec((1, rows, cols), one),
            pl.BlockSpec((1, rows, cols), one),
            pl.BlockSpec((1, 2, LANES), one),
        ],
        out_shape=[
            jax.ShapeDtypeStruct((scans, rows, cols), jnp.float32),
            jax.ShapeDtypeStruct((scans, rows, cols), jnp.float32),
            jax.ShapeDtypeStruct((scans, 2, LANES), jnp.float32),
        ],
        scratch_shapes=[
            pltpu.VMEM((scans, n_wide, rows + 2 * PAD, LANES), jnp.float32),
            pltpu.VMEM((scans, n_wide, ext, LANES), jnp.float32),
            pltpu.VMEM((n_wide, rows + 2 * EDGE, LANES), jnp.float32),
            pltpu.VMEM((rows // LANES, n_wide * LANES, LANES), jnp.float32),
            pltpu.SemaphoreType.DMA((scans, 3)),
        ],
        compiler_params=pltpu.CompilerParams(vmem_limit_bytes=VMEM_LIMIT),
        name="final",
    )(z, uc, invr, mc, mr, ac, upr, dnr)


def window_weight(index, count):
    total = jnp.zeros(index.shape, jnp.float32)
    for k in range(-SR, SR + 1):
        inside = (index + k >= 0) & (index + k < count)
        total = total + jnp.where(inside, TAPS[k + SR], 0.0)
    return total


def mean_matrix(start, length, count, width):
    fine = start + lax.broadcasted_iota(jnp.int32, (length, 1), 0)
    blocks = start // BLOCK - 1 + lax.broadcasted_iota(jnp.int32, (1, width), 1)
    valid = lax.broadcasted_iota(jnp.int32, (1, width), 1) < length // BLOCK + 2
    total = jnp.zeros((length, width), jnp.float32)
    for k in range(-SR, SR + 1):
        other = fine + k
        inside = (other >= 0) & (other < count)
        coef = jnp.where(inside, TAPS[k + SR] / (BLOCK * window_weight(other, count)), 0.0)
        total = total + jnp.where((other // BLOCK == blocks) & valid, coef, 0.0)
    return total


def mean_weights(start, length, count):
    b = BLOCK
    cases = (
        (8 * b - 8, 8), (8 * b, 8), (8 * b + 8, 8), (9 * b, 8),
        (0, -1), (0, 0), (length - 8, length // b - 1), (length - 8, length // b),
    )
    base = jnp.array([c[0] for c in cases], jnp.int32)[:, None]
    block = jnp.array([c[1] for c in cases], jnp.int32)[:, None] + start // b
    fine = start + base + jnp.arange(8, dtype=jnp.int32)[None, :]
    total = jnp.zeros(fine.shape, jnp.float32)
    for k in range(-SR, SR + 1):
        other = fine + k
        inside = (other >= 0) & (other < count) & (other // b == block)
        total = total + jnp.where(inside, TAPS[k + SR] / (b * window_weight(other, count)), 0.0)
    return jnp.broadcast_to(total.reshape(64, 1), (64, LANES))


def gauss(distance):
    scaled = (distance * BLOCK).astype(jnp.float32) / (ALPHA * LCUT)
    return jnp.exp(-math.pi * scaled * scaled)


def long_matrix(start_block, per_tile, tiles, src_ext, src_first, ext):
    count = per_tile * tiles
    i = jnp.arange(src_ext, dtype=jnp.int32)
    src = start_block - src_first + i
    src_ok = (i >= src_first - 1) & (i <= src_first + per_tile)
    e = jnp.arange(ext, dtype=jnp.int32)
    tgt = (jnp.arange(tiles, dtype=jnp.int32)[:, None] * per_tile - 1 + e[None, :]).reshape(-1)
    tgt = jnp.clip(tgt, 0, count - 1)
    norm = jnp.sum(gauss(jnp.arange(count, dtype=jnp.int32)[None, :] - tgt[:, None]), axis=1)
    m = gauss(src[None, :] - tgt[:, None]) / norm[:, None]
    return jnp.where(src_ok[None, :], m, 0.0)


def upsample_cols(per_tile, wide):
    q = lax.broadcasted_iota(jnp.int32, (LANES, wide), 1) - LANES
    num = 2 * q + 1 - BLOCK
    low = num // (2 * BLOCK)
    frac = (num - low * (2 * BLOCK)).astype(jnp.float32) / (2.0 * BLOCK)
    e = lax.broadcasted_iota(jnp.int32, (LANES, wide), 0)
    near = (q >= -1) & (q <= per_tile * BLOCK)
    m = jnp.where(e == low + 1, 1.0 - frac, 0.0) + jnp.where(e == low + 2, frac, 0.0)
    return jnp.where(near, m, 0.0).astype(jnp.bfloat16)


def in_hbm(x):
    return pltpu.with_memory_space_constraint(x, pltpu.HBM)


def body(before_scan, after_scan, drift_offsets, drift_fractions):
    scans, rows, cols = before_scan.shape
    n_row, n_col = lax.axis_size("row"), lax.axis_size("col")
    row, col = lax.axis_index("row"), lax.axis_index("col")
    offs = drift_offsets.reshape(2, scans)
    fracs = drift_fractions.reshape(2, scans)
    row_down = [(i, i + 1) for i in range(n_row - 1)]
    row_up = [(j, i) for i, j in row_down]
    col_down = [(i, i + 1) for i in range(n_col - 1)]
    col_up = [(j, i) for i, j in col_down]

    top, bot = pack(in_hbm(after_scan))
    up = lax.ppermute(bot, "row", row_down)
    dn = lax.ppermute(top, "row", row_up)
    wide = cols + 2 * LANES
    ext_r, ext_c = 24, 72
    wt = mean_weights(col * cols, cols, n_col * cols)
    rm = mean_matrix(row * rows, rows, n_row * rows, ext_r)
    rm = jnp.stack([jnp.pad(rm, ((0, 0), (s * ext_r, LANES - (s + 1) * ext_r))) for s in range(scans)])
    hc = long_matrix(col * (cols // BLOCK), cols // BLOCK, n_col, cols // BLOCK + 16, 8, ext_c)
    hr = long_matrix(row * (rows // BLOCK), rows // BLOCK, n_row, ext_r, 1, ext_r)
    uc = upsample_cols(cols // BLOCK, wide)
    qg = col * cols - EDGE + jnp.arange(cols + 2 * EDGE, dtype=jnp.int32)
    near = (qg >= col * cols - 1) & (qg <= (col + 1) * cols)
    inv = jnp.where(near, 1.0 / jnp.where(near, window_weight(qg, n_col * cols), 1.0), 0.0)
    inv = jnp.broadcast_to(inv[:, None], (cols + 2 * EDGE, LANES))
    pg = row * rows - EDGE + jnp.arange(rows + 2 * EDGE, dtype=jnp.int32)
    nearr = (pg >= row * rows - 1) & (pg <= (row + 1) * rows)
    invr = jnp.where(nearr, 1.0 / jnp.where(nearr, window_weight(pg, n_row * rows), 1.0), 0.0)
    invr = jnp.broadcast_to(invr[:, None], (rows + 2 * EDGE, LANES))
    qi = col * cols + jnp.arange(cols, dtype=jnp.int32)
    mc = ((qi >= 1) & (qi <= n_col * cols - 2)).astype(jnp.float32)[None, :]
    pi = row * rows + jnp.arange(rows, dtype=jnp.int32)
    mr = ((pi >= 1) & (pi <= n_row * rows - 2)).astype(jnp.float32)
    mr = jnp.broadcast_to(mr[:, None], (rows, LANES))

    mine = jnp.stack([offs[0], fracs[0]])
    mine, wt, rm, hc, hr, uc, inv, invr, mc, mr = lax.optimization_barrier(
        (mine, wt, rm, hc, hr, uc, inv, invr, mc, mr)
    )
    prev = lax.ppermute(mine, "col", col_down)
    following = lax.ppermute(mine, "col", col_up)
    left, right = edge_rows(prev, following, after_scan, up, dn)
    lcols = lax.ppermute(right, "col", col_down)
    rcols = lax.ppermute(left, "col", col_up)
    own = own_rows(mine, after_scan, up, dn)
    beforet = in_hbm(flip(lax.optimization_barrier((before_scan, left))[0]))
    diff, y = resample(offs, fracs, wt, rm, hc, ext_c, own, lcols, rcols, beforet)
    y = lax.all_to_all(y, "col", 0, 0, tiled=True)
    z = long_rows(y, hr, scans, ext_c)
    ac, ftop, fbot = across(inv, in_hbm(diff), y)
    upr = lax.ppermute(fbot, "row", row_down)
    dnr = lax.ppermute(ftop, "row", row_up)
    z = lax.all_to_all(z, "row", 0, 0, tiled=True)
    band, slope, sums = final(z, uc, invr, mc, mr, in_hbm(ac), upr, dnr)

    mine = jnp.sum(sums, axis=2).T.reshape(1, 2 * scans)
    mine = jnp.broadcast_to(mine[:, None, :], (n_row * n_col, 1, 2 * scans))
    every = lax.all_to_all(mine, ("row", "col"), 0, 0, tiled=True)
    total = jnp.sum(every, axis=(0, 1)).reshape(2, scans)
    cells = n_row * rows * n_col * cols
    return band, slope, jnp.sqrt(total / cells + EPSILON)


def solution(mesh):
    in_specs = (
        P(None, "row", "col"),
        P(None, "row", "col"),
        P(None, None, "row", "col"),
        P(None, None, "row", "col"),
    )
    out_specs = (P(None, "row", "col"), P(None, "row", "col"), P())
    return jax.shard_map(body, mesh=mesh, in_specs=in_specs, out_specs=out_specs, check_vma=False)
```
